256 devices in a mesh: cplx: 4 (over y_hi, core), row: 64 (over z, x, y_lo).
Axes of the slice: x: 4, y: 4 (y_hi: 2, y_lo: 2; y = y_hi * 2 + y_lo), z: 8, core: 2. Of those that a mesh axis runs over, the one named last changes fastest.
Arguments:
- pair_state: bfloat16 [2048, 512, 128], P(('cplx', 'row')), parts along dimension 0, may hold values from -60 to 60
- cotangent: bfloat16 [2048, 512, 128], P(('cplx', 'row')), parts along dimension 0, may hold values from -6 to 6
- token_mask: int32 [2048], P('cplx'), parts along dimension 0, may hold values 0 or 1
- input_gain: float32 [128], replicated, may hold values from 0.25 to 1.75
- input_bias: float32 [128], replicated, may hold values from -3 to 3
- input_weight: bfloat16 [128, 640], replicated, may hold values from -0.5 to 0.5
- output_gain: float32 [128], replicated, may hold values from 0.25 to 1.75
- output_bias: float32 [128], replicated, may hold values from -3 to 3
- output_weight: bfloat16 [128, 128], replicated, may hold values from -0.5 to 0.5
Outputs:
- pair_gradient: bfloat16 [2048, 512, 128], P(('cplx', 'row')), parts along dimension 0
- input_gradient: float32 [512, 640], P(('cplx', 'row')), parts along dimension 0
- output_gradient: float32 [512, 128], P(('cplx', 'row')), parts along dimension 0
The draws below stay inside these ranges and needn't reach their ends.
There are 4 independent parts, one for each index of `cplx`. The reference program is written for one: setup_inputs(seed, part) draws one part's arguments, and reference() takes and returns one part's arrays. A program takes and returns all parts, laid end to end along the dimension named above; an argument that names none is the same for every part. Nothing has to cross between parts.
Inputs may be any that keep to these rules, and one draw needn't show every extreme that they name: `token_mask`: 1 marks a token of the complex, 0 a padding slot.
All inputs are finite; a program needn't handle non-finite values.
Results may differ from the reference program's by a relative error of at most 0.0076.
Values may be sent and summed in bfloat16 or wider, within the bound.
No kernel may reach another device: no remote copies, remote signals or barrier semaphores. Data moves between devices by JAX's collectives and lax.ppermute only.
A program may use at most 64 MiB of HBM per device.

```python
import math
import jax
import jax.numpy as jnp
from jax import lax

C = 128
N = 512


def draw_pair_state(key, part):
    subkeys = jax.random.split(key, 8)
    random_part = jax.random.normal(subkeys[0], (N, N, C), jnp.float32)
    cell_scale = jnp.exp(jax.random.uniform(subkeys[1], (N, N, 1), jnp.float32, 0.0, math.log(10.0))) * 0.5
    channel_scale = jnp.exp(jax.random.uniform(subkeys[2], (1, 1, C), jnp.float32, -math.log(10.0), 0.0))
    offset = jax.random.normal(subkeys[3], (N, N, 1), jnp.float32) * 0.5
    values = (random_part * channel_scale + offset) * cell_scale
    values = jnp.clip(values, -60.0, 60.0)
    row_pick = jax.random.randint(subkeys[6], (2,), 0, N)
    col_pick = jax.random.randint(subkeys[7], (2,), 0, N)
    row_index = jnp.arange(N)[:, None, None]
    col_index = jnp.arange(N)[None, :, None]
    chan_index = jnp.arange(C)[None, None, :]
    top_cell = (row_index == row_pick[0]) & (col_index == col_pick[0]) & (chan_index == 0)
    low_cell = (row_index == row_pick[1]) & (col_index == col_pick[1]) & (chan_index == 1)
    values = jnp.where(top_cell, 60.0, values)
    values = jnp.where(low_cell, -60.0, values)
    return values.astype(jnp.bfloat16)


def place_ends(drawn, stream_key, least, largest):
    extent = drawn.shape
    place = [jax.random.randint(jax.random.fold_in(stream_key, axis), (), 0, extent[axis]) for axis in range(len(extent))]
    drawn = drawn.at[tuple(place)].set(least)
    longest = extent.index(max(extent))
    place[longest] = (place[longest] + 1) % extent[longest]
    return drawn.at[tuple(place)].set(largest)


def levels(own_key, dims, cuts, smallest, high):
    factor_of = 1.0
    for axis_at, blocks in cuts:
        draws = jax.random.uniform(jax.random.fold_in(jax.random.fold_in(own_key, 6), axis_at), (blocks,), jnp.float32, smallest / len(cuts), high / len(cuts))
        factor_of = factor_of * jnp.repeat(jnp.exp(draws), dims[axis_at] // blocks).reshape((-1,) + (1,) * (len(dims) - 1 - axis_at))
    return factor_of


def centred(stream_key, shape, spread, reach, cuts=(), kind=jnp.bfloat16):
    gain = levels(stream_key, shape, cuts, -0.22, 0.18) if cuts else 1.0
    entries = jax.random.normal(stream_key, shape, jnp.float32) * spread * gain
    return jnp.minimum(jnp.maximum(entries, -reach), reach).astype(kind)


def setup_inputs(seed: int = 0, part: int = 0) -> dict:
    splits = jax.random.split(jax.random.key(seed), 10)
    part_keys = jax.random.split(jax.random.fold_in(splits[9], part), 10)
    return {
        "pair_state": draw_pair_state(jax.random.fold_in(jax.random.fold_in(splits[9], part), 71), part),
        "cotangent": centred(part_keys[1], (N, N, C), 1.0, 6.0, ((0, 64),)),
        "token_mask": place_ends((jax.random.randint(part_keys[2], (N,), 0, 8) < 7).astype(jnp.int32), jax.random.fold_in(part_keys[2], 1), 0, 1),
        "input_gain": jnp.clip(1.0 + 0.15 * jax.random.normal(splits[3], (C,), jnp.float32), 0.25, 1.75),
        "input_bias": centred(splits[4], (C,), 0.5, 3.0, (), jnp.float32),
        "input_weight": centred(splits[5], (C, 5 * C), C ** -0.5, 0.5),
        "output_gain": jnp.clip(1.0 + 0.15 * jax.random.normal(splits[6], (C,), jnp.float32), 0.25, 1.75),
        "output_bias": centred(splits[7], (C,), 0.5, 3.0, (), jnp.float32),
        "output_weight": centred(splits[8], (C, C), C ** -0.5, 0.5),
    }


epsilon = 1e-05

def norm_parts(values):
    average = lax.optimization_barrier(jnp.mean(values, axis=-1, keepdims=True))
    centered = values - average
    variance = lax.optimization_barrier(jnp.mean(centered * centered, axis=-1, keepdims=True))
    inverse = lax.rsqrt(variance + epsilon)
    return (centered * inverse, inverse)

def norm_backward(upstream, scaled, inverse):
    first_mean = lax.optimization_barrier(jnp.mean(upstream, axis=-1, keepdims=True))
    second = lax.optimization_barrier(jnp.mean(upstream * scaled, axis=-1, keepdims=True))
    return inverse * (upstream - first_mean - scaled * second)

def flat_dot(left_side, right_side):
    result = jnp.dot(left_side.reshape(-1, left_side.shape[-1]), right_side, preferred_element_type=jnp.float32)
    return result.reshape(left_side.shape[:-1] + (right_side.shape[-1],))

def reference(pair_state, cotangent, token_mask, input_gain, input_bias, input_weight, output_gain, output_bias, output_weight):
    token_float = token_mask.astype(jnp.float32)
    pair_mask = (token_float[:, None] * token_float[None, :])[:, :, None]
    scaled_in, inverse_in = norm_parts(pair_state.astype(jnp.float32))
    normed = (scaled_in * input_gain + input_bias).astype(jnp.bfloat16)

    def column_block(position):
        return flat_dot(normed, input_weight[:, position * C:(position + 1) * C])
    left_lin = column_block(0)
    left_gate = jax.nn.sigmoid(column_block(1))
    right_lin = column_block(2)
    right_gate = jax.nn.sigmoid(column_block(3))
    out_gate = jax.nn.sigmoid(column_block(4))
    left_factor = (pair_mask * left_gate * left_lin).astype(jnp.bfloat16)
    right_factor = (pair_mask * right_gate * right_lin).astype(jnp.bfloat16)
    left_wide = left_factor.astype(jnp.float32)
    right_wide = right_factor.astype(jnp.float32)
    product = jnp.einsum('ikc,jkc->ijc', left_wide, right_wide).astype(jnp.bfloat16)
    scaled_out, inverse_out = norm_parts(product.astype(jnp.float32))
    normed_out = (scaled_out * output_gain + output_bias).astype(jnp.bfloat16)
    projected = flat_dot(normed_out, output_weight)
    upstream = cotangent.astype(jnp.float32)
    mixed_grad = (upstream * out_gate).astype(jnp.bfloat16)
    gate_grad = upstream * projected * out_gate * (1.0 - out_gate)
    out_norm_grad = flat_dot(mixed_grad, output_weight.T)
    product_grad = norm_backward(out_norm_grad * output_gain, scaled_out, inverse_out).astype(jnp.bfloat16)
    product_wide = product_grad.astype(jnp.float32)
    left_grad = jnp.einsum('ijc,jkc->ikc', product_wide, right_wide).astype(jnp.bfloat16)
    right_grad = jnp.einsum('ijc,ikc->jkc', product_wide, left_wide).astype(jnp.bfloat16)
    left_back = left_grad.astype(jnp.float32) * pair_mask
    right_back = right_grad.astype(jnp.float32) * pair_mask
    blocks = [(left_back * left_gate).astype(jnp.bfloat16), (left_back * left_lin * left_gate * (1.0 - left_gate)).astype(jnp.bfloat16), (right_back * right_gate).astype(jnp.bfloat16), (right_back * right_lin * right_gate * (1.0 - right_gate)).astype(jnp.bfloat16), gate_grad.astype(jnp.bfloat16)]
    normed_grad = flat_dot(blocks[0], input_weight[:, 0:C].T)
    for position in range(1, 5):
        normed_grad = normed_grad + flat_dot(blocks[position], input_weight[:, position * C:(position + 1) * C].T)
    pair_gradient = norm_backward(normed_grad * input_gain, scaled_in, inverse_in).astype(jnp.bfloat16)
    flat_normed = normed.reshape(-1, C).T
    pieces = [jnp.dot(flat_normed, piece_block.reshape(-1, C), preferred_element_type=jnp.float32) for piece_block in blocks]
    input_gradient = jnp.concatenate(pieces, axis=1) / N
    output_gradient = jnp.dot(normed_out.reshape(-1, C).T, mixed_grad.reshape(-1, C), preferred_element_type=jnp.float32) / N
    return (pair_gradient, input_gradient, output_gradient)
```

```python
import jax
import jax.numpy as jnp
from jax import lax
from jax.sharding import PartitionSpec as P

epsilon = 1e-05


def norm_parts(values, norm_axis):
    average = jnp.mean(values, axis=norm_axis, keepdims=True)
    centered = values - average
    variance = jnp.mean(centered * centered, axis=norm_axis, keepdims=True)
    inverse = lax.rsqrt(variance + epsilon)
    return (centered * inverse, inverse)


def norm_backward(upstream, scaled, inverse, norm_axis):
    first_mean = jnp.mean(upstream, axis=norm_axis, keepdims=True)
    second = jnp.mean(upstream * scaled, axis=norm_axis, keepdims=True)
    return inverse * (upstream - first_mean - scaled * second)


def to_pieces(values, slab_count):
    return values.reshape(
        slab_count, values.shape[0] // slab_count, values.shape[1], values.shape[2]
    )


def from_pieces(values):
    return values.reshape(values.shape[0] * values.shape[1], values.shape[2], values.shape[3])


def triangle(left_slab, right_slab):
    result = jnp.einsum(
        "xcik,xcjk->xcij", left_slab, right_slab, preferred_element_type=jnp.float32
    )
    return result.astype(jnp.bfloat16)


def factor_gradients(grad_slab, left_slab, right_slab):
    left_part = jnp.einsum(
        "xcij,xcjk->xcik", grad_slab, right_slab, preferred_element_type=jnp.float32
    )
    right_part = jnp.einsum(
        "xcij,xcik->xcjk", grad_slab, left_slab, preferred_element_type=jnp.float32
    )
    return (left_part.astype(jnp.bfloat16), right_part.astype(jnp.bfloat16))


def project(normed, weight_block):
    return jnp.einsum("rnd,de->ern", normed, weight_block, preferred_element_type=jnp.float32)


def on_device(
    pair_state,
    cotangent,
    token_mask,
    input_gain,
    input_bias,
    input_weight,
    output_gain,
    output_bias,
    output_weight,
):
    row_count = pair_state.shape[0]
    tokens = pair_state.shape[1]
    channels = pair_state.shape[2]
    slab_count = lax.axis_size("row")
    token_float = token_mask.astype(jnp.float32)
    row_start = lax.axis_index("row") * row_count
    row_float = lax.dynamic_slice_in_dim(token_float, row_start, row_count)
    pair_mask = (row_float[:, None] * token_float[None, :])[None]
    scaled_in, inverse_in = norm_parts(pair_state.astype(jnp.float32), 2)
    normed = (scaled_in * input_gain + input_bias).astype(jnp.bfloat16)
    left_proj = project(normed, input_weight[:, 0 : 2 * channels])
    right_proj = project(normed, input_weight[:, 2 * channels : 4 * channels])
    out_gate = jax.nn.sigmoid(project(normed, input_weight[:, 4 * channels :]))
    left_lin = left_proj[:channels]
    left_gate = jax.nn.sigmoid(left_proj[channels:])
    right_lin = right_proj[:channels]
    right_gate = jax.nn.sigmoid(right_proj[channels:])
    left_rows = to_pieces((pair_mask * left_gate * left_lin).astype(jnp.bfloat16), slab_count)
    right_rows = to_pieces((pair_mask * right_gate * right_lin).astype(jnp.bfloat16), slab_count)
    both_rows = jnp.concatenate([left_rows, right_rows], axis=1)
    both_slabs = lax.all_to_all(both_rows, "row", split_axis=0, concat_axis=2, tiled=True)
    half = channels // slab_count
    left_slab, right_slab = both_slabs[:, :half], both_slabs[:, half:]
    product_slab = triangle(left_slab, right_slab)
    product_pieces = lax.all_to_all(product_slab, "row", split_axis=2, concat_axis=0, tiled=True)
    product_rows = from_pieces(product_pieces).astype(jnp.float32)
    scaled_out, inverse_out = norm_parts(product_rows, 0)
    normed_out = (scaled_out * output_gain[:, None, None] + output_bias[:, None, None]).astype(
        jnp.bfloat16
    )
    projected = jnp.einsum(
        "crn,cd->drn", normed_out, output_weight, preferred_element_type=jnp.float32
    )
    upstream = jnp.transpose(cotangent, (2, 0, 1)).astype(jnp.float32)
    mixed_grad = (upstream * out_gate).astype(jnp.bfloat16)
    gate_grad = upstream * projected * out_gate * (1.0 - out_gate)
    out_norm_grad = jnp.einsum(
        "drn,cd->crn", mixed_grad, output_weight, preferred_element_type=jnp.float32
    )
    product_grad = norm_backward(
        out_norm_grad * output_gain[:, None, None], scaled_out, inverse_out, 0
    ).astype(jnp.bfloat16)
    grad_rows = to_pieces(product_grad, slab_count)
    grad_slab = lax.all_to_all(grad_rows, "row", split_axis=0, concat_axis=2, tiled=True)
    left_part, right_part = factor_gradients(grad_slab, left_slab, right_slab)
    both_parts = jnp.concatenate([left_part, right_part], axis=1)
    both_pieces = lax.all_to_all(both_parts, "row", split_axis=2, concat_axis=0, tiled=True)
    left_pieces, right_pieces = both_pieces[:, :half], both_pieces[:, half:]
    left_back = from_pieces(left_pieces).astype(jnp.float32) * pair_mask
    right_back = from_pieces(right_pieces).astype(jnp.float32) * pair_mask
    proj_grad = jnp.concatenate(
        [
            (left_back * left_gate).astype(jnp.bfloat16),
            (left_back * left_lin * left_gate * (1.0 - left_gate)).astype(jnp.bfloat16),
            (right_back * right_gate).astype(jnp.bfloat16),
            (right_back * right_lin * right_gate * (1.0 - right_gate)).astype(jnp.bfloat16),
            gate_grad.astype(jnp.bfloat16),
        ],
        axis=0,
    )
    normed_grad = jnp.einsum(
        "ern,de->rnd", proj_grad, input_weight, preferred_element_type=jnp.float32
    )
    pair_gradient = norm_backward(normed_grad * input_gain, scaled_in, inverse_in, 2).astype(
        jnp.bfloat16
    )
    input_term = (
        jnp.einsum("rnd,ern->de", normed, proj_grad, preferred_element_type=jnp.float32) / tokens
    )
    output_term = (
        jnp.einsum("crn,drn->cd", normed_out, mixed_grad, preferred_element_type=jnp.float32)
        / tokens
    )
    both_terms = jnp.concatenate([input_term, output_term], axis=1)
    both_terms = both_terms.reshape(slab_count, channels // slab_count, 6 * channels)
    shares = lax.all_to_all(both_terms, "row", split_axis=0, concat_axis=0, tiled=True)
    both_sums = jnp.sum(shares, axis=0)
    input_gradient = both_sums[:, : 5 * channels]
    output_gradient = both_sums[:, 5 * channels :]
    return (pair_gradient, input_gradient, output_gradient)


def solution(mesh):
    return jax.shard_map(
        on_device,
        mesh=mesh,
        in_specs=(
            P(("cplx", "row"), None, None),
            P(("cplx", "row"), None, None),
            P("cplx"),
            P(),
            P(),
            P(),
            P(),
            P(),
            P(),
        ),
        out_specs=(
            P(("cplx", "row"), None, None),
            P(("cplx", "row"), None),
            P(("cplx", "row"), None),
        ),
        check_vma=False,
    )
```

```python
import jax
import jax.numpy as jnp
from jax import lax
from jax.experimental import pallas as pl
from jax.experimental.pallas import tpu as pltpu
from jax.sharding import PartitionSpec as P

epsilon = 1e-05
LANES = 128
F32 = jnp.float32
BF16 = jnp.bfloat16


def dot_nn(a, b):
    return lax.dot_general(a, b, (((1,), (0,)), ((), ())), preferred_element_type=F32)


def dot_nt(a, b):
    return lax.dot_general(a, b, (((1,), (1,)), ((), ())), preferred_element_type=F32)


def dot_tn(a, b):
    return lax.dot_general(a, b, (((0,), (0,)), ((), ())), preferred_element_type=F32)


def eye(size, dtype):
    rows = lax.broadcasted_iota(jnp.int32, (size, size), 0)
    cols = lax.broadcasted_iota(jnp.int32, (size, size), 1)
    return jnp.where(rows == cols, 1.0, 0.0).astype(F32).astype(dtype)


def as_column(row):
    return jnp.sum(eye(row.shape[1], F32) * row, axis=1, keepdims=True)


def turned(block):
    rows, lanes, channels = block.shape
    return dot_nt(eye(channels, BF16), block.reshape(rows * lanes, channels))


def norm_columns(values):
    average = jnp.mean(values, axis=0, keepdims=True)
    centered = values - average
    variance = jnp.mean(centered * centered, axis=0, keepdims=True)
    inverse = lax.rsqrt(variance + epsilon)
    return centered * inverse, inverse


def norm_columns_backward(upstream, scaled, inverse):
    first = jnp.mean(upstream, axis=0, keepdims=True)
    second = jnp.mean(upstream * scaled, axis=0, keepdims=True)
    return inverse * (upstream - first - scaled * second)


def normed_columns(block, gain_row, bias_row):
    scaled, inverse = norm_columns(turned(block))
    normed = (scaled * as_column(gain_row) + as_column(bias_row)).astype(BF16)
    return normed, scaled, inverse


def mask_row(start_ref, mask_ref, lane_mask, rows):
    lane_float = lane_mask.astype(F32)
    parts = [
        lane_float * mask_ref[start_ref[0] + row].astype(F32) for row in range(rows)
    ]
    return jnp.concatenate(parts, axis=1)


def front_kernel(
    start_ref, mask_ref, lane_mask_ref, x_ref, gain_ref, bias_ref, weight_ref, out_ref,
    turned_weight, spread,
):
    rows = x_ref.shape[0]
    channels = x_ref.shape[2]

    @pl.when(pl.program_id(0) == 0)
    def _():
        turned_weight[...] = weight_ref[...].astype(F32).T.astype(BF16)

    normed, _, _ = normed_columns(x_ref[...], gain_ref[...], bias_ref[...])
    pair_mask = mask_row(start_ref, mask_ref, lane_mask_ref[...], rows)
    for side in range(2):
        base = 2 * side * channels
        pre = dot_nn(turned_weight[base : base + 2 * channels, :], normed)
        factor = pair_mask * jax.nn.sigmoid(pre[channels:]) * pre[:channels]
        for row in range(rows):
            spread[side, pl.ds(row, channels, stride=rows), :] = factor[
                :, row * LANES : (row + 1) * LANES
            ]
        group = channels * rows // out_ref.shape[0]
        out_ref[:, side * group : (side + 1) * group, :] = (
            spread[side].reshape(out_ref.shape[0], group, LANES).astype(BF16)
        )


def side_kernel(
    start_ref, mask_ref, lane_mask_ref, x_ref, cot_ref, gain_ref, bias_ref, weight_ref,
    out_gain_ref, out_weight_ref,
    h_ref, coef_ref, normed_ref, mixed_ref, gate_coef_ref,
    turned_weight,
):
    rows = x_ref.shape[0]
    channels = x_ref.shape[2]

    @pl.when(pl.program_id(0) == 0)
    def _():
        turned_weight[...] = weight_ref[...].astype(F32).T.astype(BF16)

    normed, _, _ = normed_columns(x_ref[...], gain_ref[...], bias_ref[...])
    normed_ref[0] = normed
    pair_mask = mask_row(start_ref, mask_ref, lane_mask_ref[...], rows)
    for side in range(2):
        base = 2 * side * channels
        pre = dot_nn(turned_weight[base : base + 2 * channels, :], normed)
        gate = jax.nn.sigmoid(pre[channels:])
        coef_ref[0, 2 * side] = pair_mask * gate
        coef_ref[0, 2 * side + 1] = pair_mask * pre[:channels] * gate * (1.0 - gate)
    out_gate = jax.nn.sigmoid(dot_nn(turned_weight[4 * channels :, :], normed))
    upstream = turned(cot_ref[...])
    mixed = (upstream * out_gate).astype(BF16)
    mixed_ref[0] = mixed
    gate_coef_ref[0] = upstream * out_gate * (1.0 - out_gate)
    h = dot_nn(out_weight_ref[...], mixed) * as_column(out_gain_ref[...])
    for row in range(rows):
        h_ref[0, pl.ds(row, channels, stride=rows), :] = h[:, row * LANES : (row + 1) * LANES]


def unpack(recv_ref, base, rows):
    block = recv_ref[:, base : base + 2 * rows, :].astype(F32)
    slabs = block.shape[0]
    return [
        block[:, part * rows : (part + 1) * rows, :].reshape(slabs * rows, LANES).astype(BF16)
        for part in range(2)
    ]


def pack(first, second, slabs):
    rows = first.shape[0] // slabs
    parts = [part.reshape(slabs, rows, LANES) for part in (first, second)]
    return jnp.concatenate(parts, axis=1).astype(BF16)


def slab_unpack_kernel(recv_ref, out_ref):
    slabs = recv_ref.shape[0]
    tokens = out_ref.shape[1]
    rows = tokens // slabs
    for tile in range(tokens // LANES):
        for side in range(2):
            parts = unpack(recv_ref, (tile * 2 + side) * 2 * rows, rows)
            for part in range(2):
                out_ref[side * 2 + part, :, tile * LANES : (tile + 1) * LANES] = parts[part]


def product_kernel(recv_ref, out_ref, slab):
    slabs = recv_ref.shape[0]
    tokens = slab.shape[1]
    slab_unpack_kernel(recv_ref, slab)
    rows = tokens // slabs
    products = [dot_nt(slab[part], slab[2 + part]) for part in range(2)]
    for tile in range(tokens // LANES):
        cols = slice(tile * LANES, (tile + 1) * LANES)
        out_ref[:, tile * 2 * rows : (tile + 1) * 2 * rows, :] = pack(
            products[0][:, cols], products[1][:, cols], slabs
        )


def product_grad_kernel(recv_ref, h_ref, out_ref):
    slabs, group, _ = recv_ref.shape
    rows = h_ref.shape[1] // (2 * slabs)
    product = recv_ref[...].astype(F32).reshape(2 * slabs, rows, LANES)
    h = h_ref[0].reshape(2 * slabs, rows, LANES)
    scaled, inverse = norm_columns(product)
    grad = norm_columns_backward(h, scaled, inverse)
    out_ref[...] = grad.reshape(slabs, group, LANES).astype(BF16)


def gather_rows(spread, channels, rows):
    return jnp.concatenate(
        [spread[pl.ds(row, channels, stride=rows), :] for row in range(rows)], axis=1
    )


def gate_side_kernel(
    recv_ref, normed_ref, mixed_ref, gate_coef_ref, out_gain_ref, out_bias_ref,
    out_weight_ref, gate_weight_ref,
    gate_normed_ref, share_ref,
    spread, gate_term, out_term, laid,
):
    step = pl.program_id(0)
    channels = normed_ref.shape[1]
    rows = normed_ref.shape[2] // LANES

    @pl.when(step == 0)
    def _():
        gate_term[...] = jnp.zeros_like(gate_term)
        out_term[...] = jnp.zeros_like(out_term)

    spread[...] = recv_ref[...].astype(F32).reshape(channels * rows, LANES)
    product = gather_rows(spread, channels, rows)
    scaled, _ = norm_columns(product)
    normed_out = (scaled * as_column(out_gain_ref[...]) + as_column(out_bias_ref[...])).astype(BF16)
    projected = dot_tn(out_weight_ref[...], normed_out)
    gate_grad = (projected * gate_coef_ref[0]).astype(BF16)
    gate_normed_ref[0] = dot_nn(gate_weight_ref[...], gate_grad)
    gate_term[...] += dot_nt(normed_ref[0], gate_grad)
    out_term[...] += dot_nt(normed_out, mixed_ref[0])

    @pl.when(step == pl.num_programs(0) - 1)
    def _():
        half = channels // 2
        for which, term in enumerate((gate_term, out_term)):
            for part in range(2):
                value = term[pl.ds(part, half, stride=2), :]
                high = value.astype(BF16).astype(F32)
                laid[pl.ds(part * 4 + which * 2, half, stride=8), :] = high
                laid[pl.ds(part * 4 + which * 2 + 1, half, stride=8), :] = value - high
        share_ref[...] = laid[...].reshape(half, 8, LANES).astype(BF16)


def factor_grad_kernel(recv_ref, factor_ref, share_ref, out_ref, slab):
    slabs = recv_ref.shape[0]
    tokens = slab.shape[1]
    rows = tokens // slabs
    for tile in range(tokens // LANES):
        parts = unpack(recv_ref, tile * 2 * rows, rows)
        for part in range(2):
            slab[part, :, tile * LANES : (tile + 1) * LANES] = parts[part]
    for side in range(2):
        if side == 0:
            grads = [dot_nn(slab[part], factor_ref[2 + part]) for part in range(2)]
        else:
            grads = [dot_tn(slab[part], factor_ref[part]) for part in range(2)]
        for tile in range(tokens // LANES):
            cols = slice(tile * LANES, (tile + 1) * LANES)
            base = (tile * 2 + side) * 2 * rows
            out_ref[:, base : base + 2 * rows, :] = pack(
                grads[0][:, cols], grads[1][:, cols], slabs
            )
    base = tokens // LANES * 4 * rows
    out_ref[:, base : base + 8, :] = share_ref[...]


def proj_grad_kernel(recv_ref, coef_ref, normed_ref, proj_ref, share_ref, spread, term):
    step = pl.program_id(0)
    channels = normed_ref.shape[1]
    rows = normed_ref.shape[2] // LANES
    group = recv_ref.shape[1] // 2

    @pl.when(step == 0)
    def _():
        term[...] = jnp.zeros_like(term)

    for side in range(2):
        spread[...] = (
            recv_ref[:, side * group : (side + 1) * group, :]
            .astype(F32)
            .reshape(channels * rows, LANES)
        )
        grad = gather_rows(spread, channels, rows)
        for part in range(2):
            block = 2 * side + part
            value = (grad * coef_ref[0, block]).astype(BF16)
            proj_ref[0, block * channels : (block + 1) * channels, :] = value
            term[block] += dot_nt(normed_ref[0], value)

    @pl.when(step == pl.num_programs(0) - 1)
    def _():
        half = channels // 2
        for part in range(2):
            for block in range(4):
                share_ref[pl.ds(part * 4 + block, half, stride=8), :] = term[
                    block, pl.ds(part, half, stride=2), :
                ]


def pair_grad_kernel(proj_ref, gate_normed_ref, x_ref, gain_ref, weight_ref, out_ref):
    rows = x_ref.shape[0]
    scaled, inverse = norm_columns(turned(x_ref[...]))
    normed_grad = dot_nn(weight_ref[...], proj_ref[0]) + gate_normed_ref[0]
    grad = norm_columns_backward(normed_grad * as_column(gain_ref[...]), scaled, inverse)
    for row in range(rows):
        out_ref[row] = grad[:, row * LANES : (row + 1) * LANES].T.astype(BF16)


def weight_sum_kernel(recv_ref, early_ref, in_ref, out_ref, *, tokens):
    late = jnp.sum(recv_ref[...], axis=0) / tokens
    early = jnp.sum(early_ref[...].astype(F32), axis=0) / tokens
    for part in range(2):
        for block in range(4):
            in_ref[part : part + 1, block * LANES : (block + 1) * LANES] = late[
                part * 4 + block : part * 4 + block + 1
            ]
        at = part * 4
        in_ref[part : part + 1, 4 * LANES :] = early[at : at + 1] + early[at + 1 : at + 2]
        out_ref[part : part + 1, :] = early[at + 2 : at + 3] + early[at + 3 : at + 4]


def whole(shape):
    return pl.BlockSpec(shape, lambda *_: (0,) * len(shape))


def exchange(values):
    return lax.all_to_all(values, "row", split_axis=0, concat_axis=0, tiled=True)


def params(**kwargs):
    return pltpu.CompilerParams(vmem_limit_bytes=56 * 1024 * 1024, **kwargs)


def cost(flops, moved):
    return pl.CostEstimate(flops=flops, bytes_accessed=moved, transcendentals=0)


def on_device(
    pair_state,
    cotangent,
    token_mask,
    input_gain,
    input_bias,
    input_weight,
    output_gain,
    output_bias,
    output_weight,
):
    rows, tokens, channels = pair_state.shape
    slabs = lax.axis_size("row")
    tiles = tokens // LANES
    cells = rows * LANES
    start = (lax.axis_index("row") * rows).astype(jnp.int32).reshape(1)
    lane_mask = token_mask.reshape(1, tokens)
    gain, bias = input_gain.reshape(1, channels), input_bias.reshape(1, channels)
    out_gain, out_bias = output_gain.reshape(1, channels), output_bias.reshape(1, channels)
    smem = pl.BlockSpec(memory_space=pltpu.SMEM)
    lane_spec = pl.BlockSpec((1, LANES), lambda t: (0, t))
    cell_spec = pl.BlockSpec((rows, LANES, channels), lambda t: (0, t, 0))
    row_spec = whole((1, channels))
    column_spec = pl.BlockSpec((1, channels, cells), lambda t: (t, 0, 0))

    def wire_spec(height):
        return pl.BlockSpec((slabs, height, LANES), lambda t: (0, t, 0))

    pair = 2 * rows
    sent_factors = pl.pallas_call(
        front_kernel,
        name="front",
        grid=(tiles,),
        in_specs=[
            smem, smem, lane_spec, cell_spec, row_spec, row_spec,
            pl.BlockSpec((channels, 4 * channels), lambda t: (0, 0)),
        ],
        out_specs=wire_spec(2 * pair),
        out_shape=jax.ShapeDtypeStruct((slabs, 2 * pair * tiles, LANES), BF16),
        scratch_shapes=[
            pltpu.VMEM((4 * channels, channels), BF16),
            pltpu.VMEM((2, channels * rows, LANES), F32),
        ],
        compiler_params=params(),
        cost_estimate=cost(6 * 10**8, 4 * 10**6),
    )(start, token_mask, lane_mask, pair_state, gain, bias, input_weight)
    factors = exchange(sent_factors)

    h, coef, normed, mixed, gate_coef = pl.pallas_call(
        side_kernel,
        name="side",
        grid=(tiles,),
        in_specs=[
            smem, smem, lane_spec, cell_spec, cell_spec, row_spec, row_spec,
            whole((channels, 5 * channels)), row_spec, whole((channels, channels)),
        ],
        out_specs=[
            pl.BlockSpec((1, channels * rows, LANES), lambda t: (t, 0, 0)),
            pl.BlockSpec((1, 4, channels, cells), lambda t: (t, 0, 0, 0)),
            column_spec, column_spec, column_spec,
        ],
        out_shape=[
            jax.ShapeDtypeStruct((tiles, channels * rows, LANES), F32),
            jax.ShapeDtypeStruct((tiles, 4, channels, cells), F32),
            jax.ShapeDtypeStruct((tiles, channels, cells), BF16),
            jax.ShapeDtypeStruct((tiles, channels, cells), BF16),
            jax.ShapeDtypeStruct((tiles, channels, cells), F32),
        ],
        scratch_shapes=[pltpu.VMEM((5 * channels, channels), BF16)],
        compiler_params=params(),
        cost_estimate=cost(12 * 10**8, 20 * 10**6),
    )(start, token_mask, lane_mask, pair_state, cotangent, gain, bias, input_weight, out_gain, output_weight)

    sent_product = pl.pallas_call(
        product_kernel,
        name="product",
        in_specs=[whole((slabs, 2 * pair * tiles, LANES))],
        out_specs=whole((slabs, pair * tiles, LANES)),
        out_shape=jax.ShapeDtypeStruct((slabs, pair * tiles, LANES), BF16),
        scratch_shapes=[pltpu.VMEM((4, tokens, tokens), BF16)],
        compiler_params=params(),
        cost_estimate=cost(6 * 10**8, 3 * 10**6),
    )(factors)
    product = exchange(sent_product)

    factor_slab = pl.pallas_call(
        slab_unpack_kernel,
        name="slabs",
        in_specs=[whole((slabs, 2 * pair * tiles, LANES))],
        out_specs=whole((4, tokens, tokens)),
        out_shape=jax.ShapeDtypeStruct((4, tokens, tokens), BF16),
        compiler_params=params(),
        cost_estimate=cost(10**6, 4 * 10**6),
    )(factors)

    sent_grad = pl.pallas_call(
        product_grad_kernel,
        name="product_grad",
        grid=(tiles,),
        in_specs=[wire_spec(pair), pl.BlockSpec((1, channels * rows, LANES), lambda t: (t, 0, 0))],
        out_specs=wire_spec(pair),
        out_shape=jax.ShapeDtypeStruct((slabs, pair * tiles, LANES), BF16),
        compiler_params=params(),
        cost_estimate=cost(10**7, 4 * 10**6),
    )(product, h)
    grad = exchange(sent_grad)

    gate_normed, early_share = pl.pallas_call(
        gate_side_kernel,
        name="gate_side",
        grid=(tiles,),
        in_specs=[
            wire_spec(pair), column_spec, column_spec, column_spec, row_spec, row_spec,
            whole((channels, channels)),
            pl.BlockSpec((channels, channels), lambda t: (0, 4)),
        ],
        out_specs=[column_spec, whole((slabs, 8, LANES))],
        out_shape=[
            jax.ShapeDtypeStruct((tiles, channels, cells), F32),
            jax.ShapeDtypeStruct((slabs, 8, LANES), BF16),
        ],
        scratch_shapes=[
            pltpu.VMEM((channels * rows, LANES), F32),
            pltpu.VMEM((channels, channels), F32),
            pltpu.VMEM((channels, channels), F32),
            pltpu.VMEM((slabs * 8, LANES), F32),
        ],
        compiler_params=params(),
        cost_estimate=cost(6 * 10**8, 8 * 10**6),
    )(product, normed, mixed, gate_coef, out_gain, out_bias, output_weight, input_weight)

    height = 2 * pair * tiles + 8
    sent_parts = pl.pallas_call(
        factor_grad_kernel,
        name="factor_grad",
        in_specs=[
            whole((slabs, pair * tiles, LANES)),
            whole((4, tokens, tokens)),
            whole((slabs, 8, LANES)),
        ],
        out_specs=whole((slabs, height, LANES)),
        out_shape=jax.ShapeDtypeStruct((slabs, height, LANES), BF16),
        scratch_shapes=[pltpu.VMEM((2, tokens, tokens), BF16)],
        compiler_params=params(),
        cost_estimate=cost(11 * 10**8, 5 * 10**6),
    )(grad, factor_slab, early_share)
    parts = exchange(sent_parts)

    proj, late_share = pl.pallas_call(
        proj_grad_kernel,
        name="proj_grad",
        grid=(tiles,),
        in_specs=[
            wire_spec(2 * pair),
            pl.BlockSpec((1, 4, channels, cells), lambda t: (t, 0, 0, 0)),
            column_spec,
        ],
        out_specs=[
            pl.BlockSpec((1, 4 * channels, cells), lambda t: (t, 0, 0)),
            whole((slabs * 8, LANES)),
        ],
        out_shape=[
            jax.ShapeDtypeStruct((tiles, 4 * channels, cells), BF16),
            jax.ShapeDtypeStruct((slabs * 8, LANES), F32),
        ],
        scratch_shapes=[
            pltpu.VMEM((channels * rows, LANES), F32),
            pltpu.VMEM((4, channels, channels), F32),
        ],
        compiler_params=params(),
        cost_estimate=cost(6 * 10**8, 15 * 10**6),
    )(parts, coef, normed)
    late = exchange(late_share.reshape(slabs, 8, LANES))

    pair_gradient = pl.pallas_call(
        pair_grad_kernel,
        name="pair_grad",
        grid=(tiles,),
        in_specs=[
            pl.BlockSpec((1, 4 * channels, cells), lambda t: (t, 0, 0)),
            column_spec, cell_spec, row_spec,
            pl.BlockSpec((channels, 4 * channels), lambda t: (0, 0)),
        ],
        out_specs=cell_spec,
        out_shape=jax.ShapeDtypeStruct((rows, tokens, channels), BF16),
        compiler_params=params(),
        cost_estimate=cost(6 * 10**8, 8 * 10**6),
    )(proj, gate_normed, pair_state, gain, input_weight)

    last = 2 * pair * tiles // 8
    held = channels // slabs
    input_gradient, output_gradient = pl.pallas_call(
        lambda *refs: weight_sum_kernel(*refs, tokens=tokens),
        name="weight_sum",
        grid=(1,),
        in_specs=[whole((slabs, 8, LANES)), pl.BlockSpec((slabs, 8, LANES), lambda t: (0, last, 0))],
        out_specs=[whole((held, 5 * channels)), whole((held, channels))],
        out_shape=[
            jax.ShapeDtypeStruct((held, 5 * channels), F32),
            jax.ShapeDtypeStruct((held, channels), F32),
        ],
        compiler_params=params(),
        cost_estimate=cost(10**5, 4 * 10**5),
    )(late, parts)
    return (pair_gradient, input_gradient, output_gradient)


def solution(mesh):
    return jax.shard_map(
        on_device,
        mesh=mesh,
        in_specs=(
            P(("cplx", "row"), None, None),
            P(("cplx", "row"), None, None),
            P("cplx"),
            P(),
            P(),
            P(),
            P(),
            P(),
            P(),
        ),
        out_specs=(
            P(("cplx", "row"), None, None),
            P(("cplx", "row"), None),
            P(("cplx", "row"), None),
        ),
        check_vma=False,
    )
```

```python
import jax
import jax.numpy as jnp
from jax import lax
from jax.experimental import pallas as pl
from jax.experimental.pallas import tpu as pltpu
from jax.sharding import PartitionSpec as P

epsilon = 1e-05
LANES = 128
F32 = jnp.float32
BF16 = jnp.bfloat16


def dot_nn(a, b):
    return lax.dot_general(a, b, (((1,), (0,)), ((), ())), preferred_element_type=F32)


def dot_nt(a, b):
    return lax.dot_general(a, b, (((1,), (1,)), ((), ())), preferred_element_type=F32)


def dot_tn(a, b):
    return lax.dot_general(a, b, (((0,), (0,)), ((), ())), preferred_element_type=F32)


def eye(size, dtype):
    rows = lax.broadcasted_iota(jnp.int32, (size, size), 0)
    cols = lax.broadcasted_iota(jnp.int32, (size, size), 1)
    return jnp.where(rows == cols, 1.0, 0.0).astype(F32).astype(dtype)


def as_column(row):
    return jnp.sum(eye(row.shape[1], F32) * row, axis=1, keepdims=True)


def turned(block):
    rows, lanes, channels = block.shape
    return dot_nt(eye(channels, BF16), block.reshape(rows * lanes, channels))


def norm_columns(values):
    average = jnp.mean(values, axis=0, keepdims=True)
    centered = values - average
    variance = jnp.mean(centered * centered, axis=0, keepdims=True)
    inverse = lax.rsqrt(variance + epsilon)
    return centered * inverse, inverse


def norm_columns_backward(upstream, scaled, inverse):
    first = jnp.mean(upstream, axis=0, keepdims=True)
    second = jnp.mean(upstream * scaled, axis=0, keepdims=True)
    return inverse * (upstream - first - scaled * second)


def normed_columns(block, gain_row, bias_row):
    scaled, inverse = norm_columns(turned(block))
    normed = (scaled * as_column(gain_row) + as_column(bias_row)).astype(BF16)
    return normed, scaled, inverse


def mask_row(start_ref, mask_ref, lane_mask, rows):
    lane_float = lane_mask.astype(F32)
    parts = [
        lane_float * mask_ref[start_ref[0] + row].astype(F32) for row in range(rows)
    ]
    return jnp.concatenate(parts, axis=1)


def front_kernel(
    start_ref, mask_ref, lane_mask_ref, x_ref, gain_ref, bias_ref, weight_ref, out_ref,
    turned_weight, spread,
):
    rows = x_ref.shape[0]
    channels = x_ref.shape[2]

    @pl.when(pl.program_id(0) == 0)
    def _():
        turned_weight[...] = weight_ref[...].astype(F32).T.astype(BF16)

    gain, bias = as_column(gain_ref[...]), as_column(bias_ref[...])
    lane_mask = lane_mask_ref[...].astype(F32)
    scaled, _ = norm_columns(turned(x_ref[...]))
    normed = (scaled * gain + bias).astype(BF16)
    masks = [lane_mask * mask_ref[start_ref[0] + row].astype(F32) for row in range(rows)]
    pair_mask = jnp.concatenate(masks, axis=1)
    for side in range(2):
        base = 2 * side * channels
        pre = dot_nn(turned_weight[base : base + 2 * channels, :], normed)
        factor = pair_mask * jax.nn.sigmoid(pre[channels:]) * pre[:channels]
        for row in range(rows):
            spread[side, pl.ds(row, channels, stride=rows), :] = factor[
                :, row * LANES : (row + 1) * LANES
            ]
    group = channels * rows // out_ref.shape[0]
    for side in range(2):
        out_ref[:, side * group : (side + 1) * group, :] = (
            spread[side].reshape(out_ref.shape[0], group, LANES).astype(BF16)
        )


def side_kernel(
    start_ref, mask_ref, lane_mask_ref, x_ref, cot_ref, gain_ref, bias_ref, weight_ref,
    out_gain_ref, out_weight_ref,
    h_ref, coef_ref, normed_ref, mixed_ref, gate_coef_ref,
    turned_weight, spread,
):
    rows = x_ref.shape[0]
    channels = x_ref.shape[2]

    @pl.when(pl.program_id(0) == 0)
    def _():
        turned_weight[...] = weight_ref[...].astype(F32).T.astype(BF16)

    normed, _, _ = normed_columns(x_ref[...], gain_ref[...], bias_ref[...])
    normed_ref[0] = normed
    pair_mask = mask_row(start_ref, mask_ref, lane_mask_ref[...], rows)
    for side in range(2):
        base = 2 * side * channels
        pre = dot_nn(turned_weight[base : base + 2 * channels, :], normed)
        gate = jax.nn.sigmoid(pre[channels:])
        coef_ref[0, 2 * side] = (pair_mask * gate).astype(BF16)
        slope = pair_mask * pre[:channels] * gate * (1.0 - gate)
        coef_ref[0, 2 * side + 1] = slope.astype(BF16)
    out_gate = jax.nn.sigmoid(dot_nn(turned_weight[4 * channels :, :], normed))
    upstream = turned(cot_ref[...])
    mixed = (upstream * out_gate).astype(BF16)
    mixed_ref[0] = mixed
    gate_coef_ref[0] = upstream * out_gate * (1.0 - out_gate)
    h = dot_nn(out_weight_ref[...], mixed) * as_column(out_gain_ref[...])
    h = h - jnp.mean(h, axis=0, keepdims=True)
    for row in range(rows):
        spread[pl.ds(row, channels, stride=rows), :] = h[:, row * LANES : (row + 1) * LANES]
    h_ref[0] = spread[...].astype(BF16)


def unpack(recv_ref, base, rows):
    block = recv_ref[:, base : base + 2 * rows, :].astype(F32)
    slabs = block.shape[0]
    return [
        block[:, part * rows : (part + 1) * rows, :].reshape(slabs * rows, LANES).astype(BF16)
        for part in range(2)
    ]


def pack(first, second, slabs):
    rows = first.shape[0] // slabs
    parts = [part.reshape(slabs, rows, LANES) for part in (first, second)]
    return jnp.concatenate(parts, axis=1).astype(BF16)


def slab_unpack_kernel(recv_ref, out_ref):
    slabs = recv_ref.shape[0]
    tokens = out_ref.shape[1]
    rows = tokens // slabs
    for tile in range(tokens // LANES):
        for side in range(2):
            parts = unpack(recv_ref, (tile * 2 + side) * 2 * rows, rows)
            for part in range(2):
                out_ref[side * 2 + part, :, tile * LANES : (tile + 1) * LANES] = parts[part]


def product_kernel(recv_ref, out_ref, slab):
    slabs = recv_ref.shape[0]
    tokens = slab.shape[1]
    slab_unpack_kernel(recv_ref, slab)
    rows = tokens // slabs
    products = [dot_nt(slab[part], slab[2 + part]) for part in range(2)]
    for tile in range(tokens // LANES):
        cols = slice(tile * LANES, (tile + 1) * LANES)
        out_ref[:, tile * 2 * rows : (tile + 1) * 2 * rows, :] = pack(
            products[0][:, cols], products[1][:, cols], slabs
        )


def product_grad_kernel(recv_ref, h_ref, factor_hbm, out_ref):
    del factor_hbm
    slabs, group, _ = out_ref.shape
    rows = group // 2
    channels = 2 * slabs
    base = pl.multiple_of(pl.program_id(0) * group, group)
    chunk = 8

    def product_at(at):
        block = recv_ref[at : at + chunk, pl.ds(base, group), :].astype(F32)
        return block.reshape(2 * chunk, rows, LANES)

    def h_at(at):
        size = 2 * chunk * rows
        block = h_ref[0, at * group : at * group + size, :].astype(F32)
        return block.reshape(2 * chunk, rows, LANES)

    total = jnp.zeros((rows, LANES), F32)
    for at in range(0, slabs, chunk):
        total = total + jnp.sum(product_at(at), axis=0)
    average = (total / channels)[None]
    squares = jnp.zeros((rows, LANES), F32)
    cross = jnp.zeros((rows, LANES), F32)
    for at in range(0, slabs, chunk):
        centered = product_at(at) - average
        squares = squares + jnp.sum(centered * centered, axis=0)
        cross = cross + jnp.sum(centered * h_at(at), axis=0)
    inverse = lax.rsqrt(squares / channels + epsilon)
    slope = (inverse * inverse * inverse * (cross / channels))[None]
    inverse = inverse[None]
    for at in range(0, slabs, chunk):
        grad = inverse * h_at(at) - (product_at(at) - average) * slope
        out_ref[at : at + chunk] = grad.reshape(chunk, group, LANES).astype(BF16)


def gather_rows(spread, channels, rows):
    return jnp.concatenate(
        [spread[pl.ds(row, channels, stride=rows), :] for row in range(rows)], axis=1
    )


def gate_side_kernel(
    recv_ref, normed_ref, mixed_ref, gate_coef_ref, out_gain_ref, out_bias_ref,
    out_weight_ref, gate_weight_ref,
    gate_normed_ref, share_ref,
    spread, gate_term, out_term, laid,
):
    step = pl.program_id(0)
    channels = normed_ref.shape[1]
    rows = normed_ref.shape[2] // LANES
    group = channels * rows // recv_ref.shape[0]
    block = recv_ref[:, pl.ds(pl.multiple_of(step * group, group), group), :]

    @pl.when(step == 0)
    def _():
        gate_term[...] = jnp.zeros_like(gate_term)
        out_term[...] = jnp.zeros_like(out_term)

    spread[...] = block.astype(F32).reshape(channels * rows, LANES)
    product = gather_rows(spread, channels, rows)
    scaled, _ = norm_columns(product)
    normed_out = (scaled * as_column(out_gain_ref[...]) + as_column(out_bias_ref[...])).astype(BF16)
    projected = dot_tn(out_weight_ref[...], normed_out)
    gate_grad = (projected * gate_coef_ref[0]).astype(BF16)
    gate_normed_ref[0] = dot_nn(gate_weight_ref[...], gate_grad)
    gate_term[...] += dot_nt(normed_ref[0], gate_grad)
    out_term[...] += dot_nt(normed_out, mixed_ref[0])

    @pl.when(step == pl.num_programs(0) - 1)
    def _():
        half = channels // 2
        for which, term in enumerate((gate_term, out_term)):
            for part in range(2):
                value = term[pl.ds(part, half, stride=2), :]
                high = value.astype(BF16).astype(F32)
                laid[pl.ds(part * 4 + which * 2, half, stride=8), :] = high
                laid[pl.ds(part * 4 + which * 2 + 1, half, stride=8), :] = value - high
        share_ref[...] = laid[...].reshape(half, 8, LANES).astype(BF16)


def factor_grad_kernel(recv_ref, factor_hbm, share_ref, out_ref, slab, factor, arrived):
    slabs = recv_ref.shape[0]
    tokens = slab.shape[1]
    rows = tokens // slabs
    loads = [
        pltpu.make_async_copy(factor_hbm.at[which], factor.at[which], arrived.at[which])
        for which in range(4)
    ]
    for which in (2, 3, 0, 1):
        loads[which].start()
    for tile in range(tokens // LANES):
        parts = unpack(recv_ref, tile * 2 * rows, rows)
        for part in range(2):
            slab[part, :, tile * LANES : (tile + 1) * LANES] = parts[part]
    for side in range(2):
        grads = []
        for part in range(2):
            which = 2 + part if side == 0 else part
            loads[which].wait()
            dot = dot_nn if side == 0 else dot_tn
            grads.append(dot(slab[part], factor[which]))
        for tile in range(tokens // LANES):
            cols = slice(tile * LANES, (tile + 1) * LANES)
            base = (tile * 2 + side) * 2 * rows
            out_ref[:, base : base + 2 * rows, :] = pack(
                grads[0][:, cols], grads[1][:, cols], slabs
            )
    base = tokens // LANES * 4 * rows
    out_ref[:, base : base + 8, :] = share_ref[...]


def proj_blocks(recv_ref, coef_ref, spread, rows):
    step = pl.program_id(0)
    channels = coef_ref.shape[2]
    group = channels * rows // recv_ref.shape[0]
    base = pl.multiple_of(step * 2 * group, 2 * group)
    for side in range(2):
        spread[side] = (
            recv_ref[:, pl.ds(base + side * group, group), :]
            .astype(F32)
            .reshape(channels * rows, LANES)
        )
    blocks = []
    for side in range(2):
        grad = gather_rows(spread.at[side], channels, rows)
        for part in range(2):
            blocks.append((grad * coef_ref[0, 2 * side + part].astype(F32)).astype(BF16))
    return blocks


def proj_grad_kernel(recv_ref, coef_ref, normed_ref, share_ref, spread, term):
    step = pl.program_id(0)
    channels = normed_ref.shape[1]
    rows = normed_ref.shape[2] // LANES

    @pl.when(step == 0)
    def _():
        term[...] = jnp.zeros_like(term)

    for block, value in enumerate(proj_blocks(recv_ref, coef_ref, spread, rows)):
        term[block] += dot_nt(normed_ref[0], value)

    @pl.when(step == pl.num_programs(0) - 1)
    def _():
        half = channels // 2
        for part in range(2):
            for block in range(4):
                share_ref[pl.ds(part * 4 + block, half, stride=8), :] = term[
                    block, pl.ds(part, half, stride=2), :
                ]


def pair_grad_kernel(
    recv_ref, coef_ref, gate_normed_ref, x_ref, gain_ref, weight_ref, out_ref, spread
):
    rows = x_ref.shape[0]
    blocks = proj_blocks(recv_ref, coef_ref, spread, rows)
    scaled, inverse = norm_columns(turned(x_ref[...]))
    normed_grad = dot_nn(weight_ref[...], jnp.concatenate(blocks, axis=0)) + gate_normed_ref[0]
    grad = norm_columns_backward(normed_grad * as_column(gain_ref[...]), scaled, inverse)
    for row in range(rows):
        out_ref[row] = grad[:, row * LANES : (row + 1) * LANES].T.astype(BF16)


def weight_sum_kernel(recv_ref, early_ref, in_ref, out_ref, *, tokens):
    last = early_ref.shape[1] - 8
    late = jnp.sum(recv_ref[...], axis=0) / tokens
    early = jnp.sum(early_ref[:, last:, :].astype(F32), axis=0) / tokens
    for part in range(2):
        for block in range(4):
            in_ref[part : part + 1, block * LANES : (block + 1) * LANES] = late[
                part * 4 + block : part * 4 + block + 1
            ]
        at = part * 4
        in_ref[part : part + 1, 4 * LANES :] = early[at : at + 1] + early[at + 1 : at + 2]
        out_ref[part : part + 1, :] = early[at + 2 : at + 3] + early[at + 3 : at + 4]


def whole(shape):
    return pl.BlockSpec(shape, lambda *_: (0,) * len(shape))


def exchange(values):
    return lax.all_to_all(values, "row", split_axis=0, concat_axis=0, tiled=True)


def params(megabytes):
    return pltpu.CompilerParams(vmem_limit_bytes=megabytes * 1024 * 1024)


def pinned(*arrays):
    return [pltpu.with_memory_space_constraint(array, pltpu.HBM) for array in arrays]


def cost(flops, moved):
    return pl.CostEstimate(flops=flops, bytes_accessed=moved, transcendentals=0)


def on_device(
    pair_state,
    cotangent,
    token_mask,
    input_gain,
    input_bias,
    input_weight,
    output_gain,
    output_bias,
    output_weight,
):
    rows, tokens, channels = pair_state.shape
    slabs = lax.axis_size("row")
    tiles = tokens // LANES
    cells = rows * LANES
    start = (lax.axis_index("row") * rows).astype(jnp.int32).reshape(1)
    lane_mask = token_mask.reshape(1, tokens)
    gain, bias = input_gain.reshape(1, channels), input_bias.reshape(1, channels)
    out_gain, out_bias = output_gain.reshape(1, channels), output_bias.reshape(1, channels)
    smem = pl.BlockSpec(memory_space=pltpu.SMEM)
    lane_spec = pl.BlockSpec((1, LANES), lambda t: (0, t))
    cell_spec = pl.BlockSpec((rows, LANES, channels), lambda t: (0, t, 0))
    row_spec = whole((1, channels))
    column_spec = pl.BlockSpec((1, channels, cells), lambda t: (t, 0, 0))

    def wire_spec(height):
        return pl.BlockSpec((slabs, height, LANES), lambda t: (0, t, 0))

    pair = 2 * rows
    vmem = pl.BlockSpec(memory_space=pltpu.VMEM)
    h_spec = pl.BlockSpec((1, channels * rows, LANES), lambda t: (t, 0, 0))
    coef_spec = pl.BlockSpec((1, 4, channels, cells), lambda t: (t, 0, 0, 0))
    factor_weight_spec = pl.BlockSpec((channels, 4 * channels), lambda t: (0, 0))
    pair_hbm, cot_hbm, lane_hbm, gain, bias, out_gain, out_bias, weight, out_weight = pinned(
        pair_state, cotangent, lane_mask, gain, bias, out_gain, out_bias, input_weight, output_weight
    )

    sent_factors = pl.pallas_call(
        front_kernel,
        name="front",
        grid=(tiles,),
        in_specs=[
            smem, smem, lane_spec, cell_spec, row_spec, row_spec, factor_weight_spec,
        ],
        out_specs=wire_spec(2 * pair),
        out_shape=jax.ShapeDtypeStruct((slabs, 2 * pair * tiles, LANES), BF16),
        scratch_shapes=[
            pltpu.VMEM((4 * channels, channels), BF16),
            pltpu.VMEM((2, channels * rows, LANES), F32),
        ],
        compiler_params=params(16),
        cost_estimate=cost(6 * 10**8, 4 * 10**6),
    )(start, token_mask, lane_hbm, pair_hbm, gain, bias, weight)
    factors = exchange(sent_factors)

    h, coef, normed, mixed, gate_coef = pl.pallas_call(
        side_kernel,
        name="side",
        grid=(tiles,),
        in_specs=[
            smem, smem, lane_spec, cell_spec, cell_spec, row_spec, row_spec,
            whole((channels, 5 * channels)), row_spec, whole((channels, channels)),
        ],
        out_specs=[h_spec, coef_spec, column_spec, column_spec, column_spec],
        out_shape=[
            pltpu.HBM((tiles, channels * rows, LANES), BF16),
            pltpu.HBM((tiles, 4, channels, cells), BF16),
            pltpu.HBM((tiles, channels, cells), BF16),
            pltpu.HBM((tiles, channels, cells), BF16),
            pltpu.HBM((tiles, channels, cells), F32),
        ],
        scratch_shapes=[
            pltpu.VMEM((5 * channels, channels), BF16),
            pltpu.VMEM((channels * rows, LANES), F32),
        ],
        compiler_params=params(40),
        cost_estimate=cost(12 * 10**8, 16 * 10**6),
    )(start, token_mask, lane_hbm, pair_hbm, cot_hbm, gain, bias, weight, out_gain, out_weight)
    h, coef, normed, mixed, gate_coef = pinned(h, coef, normed, mixed, gate_coef)

    sent_product = pl.pallas_call(
        product_kernel,
        name="product",
        in_specs=[vmem],
        out_specs=whole((slabs, pair * tiles, LANES)),
        out_shape=pltpu.HBM((slabs, pair * tiles, LANES), BF16),
        scratch_shapes=[pltpu.VMEM((4, tokens, tokens), BF16)],
        compiler_params=params(20),
        cost_estimate=cost(6 * 10**8, 3 * 10**6),
    )(factors)
    product = exchange(sent_product)

    factor_slab = pl.pallas_call(
        slab_unpack_kernel,
        name="slabs",
        in_specs=[vmem],
        out_specs=whole((4, tokens, tokens)),
        out_shape=pltpu.HBM((4, tokens, tokens), BF16),
        compiler_params=params(20),
        cost_estimate=cost(10**6, 4 * 10**6),
    )(factors)
    (factor_slab,) = pinned(factor_slab)

    sent_grad = pl.pallas_call(
        product_grad_kernel,
        name="product_grad",
        grid=(tiles,),
        in_specs=[vmem, h_spec, pl.BlockSpec(memory_space=pl.ANY)],
        out_specs=wire_spec(pair),
        out_shape=pltpu.HBM((slabs, pair * tiles, LANES), BF16),
        compiler_params=params(16),
        cost_estimate=cost(10**7, 4 * 10**6),
    )(product, h, factor_slab)
    grad = exchange(sent_grad)

    gate_normed, early_share = pl.pallas_call(
        gate_side_kernel,
        name="gate_side",
        grid=(tiles,),
        in_specs=[
            vmem, column_spec, column_spec, column_spec, row_spec, row_spec,
            whole((channels, channels)),
            pl.BlockSpec((channels, channels), lambda t: (0, 4)),
        ],
        out_specs=[column_spec, whole((slabs, 8, LANES))],
        out_shape=[
            pltpu.HBM((tiles, channels, cells), F32),
            pltpu.HBM((slabs, 8, LANES), BF16),
        ],
        scratch_shapes=[
            pltpu.VMEM((channels * rows, LANES), F32),
            pltpu.VMEM((channels, channels), F32),
            pltpu.VMEM((channels, channels), F32),
            pltpu.VMEM((slabs * 8, LANES), F32),
        ],
        compiler_params=params(24),
        cost_estimate=cost(6 * 10**8, 8 * 10**6),
    )(product, normed, mixed, gate_coef, out_gain, out_bias, out_weight, weight)
    gate_normed, early_share = pinned(gate_normed, early_share)

    height = 2 * pair * tiles + 8
    sent_parts = pl.pallas_call(
        factor_grad_kernel,
        name="factor_grad",
        in_specs=[vmem, pl.BlockSpec(memory_space=pl.ANY), whole((slabs, 8, LANES))],
        out_specs=vmem,
        out_shape=jax.ShapeDtypeStruct((slabs, height, LANES), BF16),
        scratch_shapes=[
            pltpu.VMEM((2, tokens, tokens), BF16),
            pltpu.VMEM((4, tokens, tokens), BF16),
            pltpu.SemaphoreType.DMA((4,)),
        ],
        compiler_params=params(20),
        cost_estimate=cost(11 * 10**8, 5 * 10**6),
    )(grad, factor_slab, early_share)
    parts = exchange(sent_parts)

    late_share = pl.pallas_call(
        proj_grad_kernel,
        name="proj_grad",
        grid=(tiles,),
        in_specs=[vmem, coef_spec, column_spec],
        out_specs=whole((slabs * 8, LANES)),
        out_shape=pltpu.HBM((slabs * 8, LANES), F32),
        scratch_shapes=[
            pltpu.VMEM((2, channels * rows, LANES), F32),
            pltpu.VMEM((4, channels, channels), F32),
        ],
        compiler_params=params(24),
        cost_estimate=cost(6 * 10**8, 8 * 10**6),
    )(parts, coef, normed)
    late = exchange(late_share.reshape(slabs, 8, LANES))

    pair_gradient = pl.pallas_call(
        pair_grad_kernel,
        name="pair_grad",
        grid=(tiles,),
        in_specs=[vmem, coef_spec, column_spec, cell_spec, row_spec, factor_weight_spec],
        out_specs=cell_spec,
        out_shape=pltpu.HBM((rows, tokens, channels), BF16),
        scratch_shapes=[pltpu.VMEM((2, channels * rows, LANES), F32)],
        compiler_params=params(24),
        cost_estimate=cost(6 * 10**8, 8 * 10**6),
    )(parts, coef, gate_normed, pair_hbm, gain, weight)

    held = channels // slabs
    input_gradient, output_gradient = pl.pallas_call(
        lambda *refs: weight_sum_kernel(*refs, tokens=tokens),
        name="weight_sum",
        in_specs=[vmem, vmem],
        out_specs=[whole((held, 5 * channels)), whole((held, channels))],
        out_shape=[
            pltpu.HBM((held, 5 * channels), F32),
            pltpu.HBM((held, channels), F32),
        ],
        compiler_params=params(16),
        cost_estimate=cost(10**5, 4 * 10**5),
    )(late, parts)
    return (pair_gradient, input_gradient, output_gradient)


def solution(mesh):
    return jax.shard_map(
        on_device,
        mesh=mesh,
        in_specs=(
            P(("cplx", "row"), None, None),
            P(("cplx", "row"), None, None),
            P("cplx"),
            P(),
            P(),
            P(),
            P(),
            P(),
            P(),
        ),
        out_specs=(
            P(("cplx", "row"), None, None),
            P(("cplx", "row"), None),
            P(("cplx", "row"), None),
        ),
        check_vma=False,
    )
```

```python
import jax
import jax.numpy as jnp
from jax import lax
from jax.experimental import pallas as pl
from jax.experimental.pallas import tpu as pltpu
from jax.sharding import PartitionSpec as P

epsilon = 1e-05
LANES = 128
F32 = jnp.float32
BF16 = jnp.bfloat16


def dot_nn(a, b):
    return lax.dot_general(a, b, (((1,), (0,)), ((), ())), preferred_element_type=F32)


def dot_nt(a, b):
    return lax.dot_general(a, b, (((1,), (1,)), ((), ())), preferred_element_type=F32)


def dot_tn(a, b):
    return lax.dot_general(a, b, (((0,), (0,)), ((), ())), preferred_element_type=F32)


def eye(size, dtype):
    rows = lax.broadcasted_iota(jnp.int32, (size, size), 0)
    cols = lax.broadcasted_iota(jnp.int32, (size, size), 1)
    return jnp.where(rows == cols, 1.0, 0.0).astype(F32).astype(dtype)


def as_column(row):
    return jnp.sum(eye(row.shape[1], F32) * row, axis=1, keepdims=True)


def turned(block):
    rows, lanes, channels = block.shape
    return dot_nt(eye(channels, BF16), block.reshape(rows * lanes, channels))


def norm_columns(values):
    average = jnp.mean(values, axis=0, keepdims=True)
    centered = values - average
    variance = jnp.mean(centered * centered, axis=0, keepdims=True)
    inverse = lax.rsqrt(variance + epsilon)
    return centered * inverse, inverse


def norm_columns_backward(upstream, scaled, inverse):
    first = jnp.mean(upstream, axis=0, keepdims=True)
    second = jnp.mean(upstream * scaled, axis=0, keepdims=True)
    return inverse * (upstream - first - scaled * second)


def normed_columns(block, gain_row, bias_row):
    scaled, inverse = norm_columns(turned(block))
    normed = (scaled * as_column(gain_row) + as_column(bias_row)).astype(BF16)
    return normed, scaled, inverse


def mask_row(start_ref, mask_ref, lane_mask, rows):
    lane_float = lane_mask.astype(F32)
    parts = [
        lane_float * mask_ref[start_ref[0] + row].astype(F32) for row in range(rows)
    ]
    return jnp.concatenate(parts, axis=1)


def front_kernel(
    start_ref, mask_ref, lane_mask_ref, x_ref, gain_ref, bias_ref, weight_ref, out_ref,
    turned_weight, spread,
):
    rows = x_ref.shape[0]
    channels = x_ref.shape[2]

    @pl.when(pl.program_id(0) == 0)
    def _():
        turned_weight[...] = weight_ref[...].astype(F32).T.astype(BF16)

    gain, bias = as_column(gain_ref[...]), as_column(bias_ref[...])
    lane_mask = lane_mask_ref[...].astype(F32)
    scaled, _ = norm_columns(turned(x_ref[...]))
    normed = (scaled * gain + bias).astype(BF16)
    masks = [lane_mask * mask_ref[start_ref[0] + row].astype(F32) for row in range(rows)]
    pair_mask = jnp.concatenate(masks, axis=1)
    for side in range(2):
        base = 2 * side * channels
        pre = dot_nn(turned_weight[base : base + 2 * channels, :], normed)
        factor = pair_mask * jax.nn.sigmoid(pre[channels:]) * pre[:channels]
        for row in range(rows):
            spread[side, pl.ds(row, channels, stride=rows), :] = factor[
                :, row * LANES : (row + 1) * LANES
            ]
    group = channels * rows // out_ref.shape[0]
    for side in range(2):
        out_ref[:, side * group : (side + 1) * group, :] = (
            spread[side].reshape(out_ref.shape[0], group, LANES).astype(BF16)
        )


def side_kernel(
    start_ref, mask_ref, lane_mask_ref, x_ref, cot_ref, gain_ref, bias_ref, weight_ref,
    out_gain_ref, out_weight_ref,
    h_ref, coef_ref, normed_ref, mixed_ref, gate_coef_ref,
    turned_weight,
):
    rows = x_ref.shape[0]
    channels = x_ref.shape[2]

    @pl.when(pl.program_id(0) == 0)
    def _():
        turned_weight[...] = weight_ref[...].astype(F32).T.astype(BF16)

    normed, _, _ = normed_columns(x_ref[...], gain_ref[...], bias_ref[...])
    normed_ref[0] = normed
    pair_mask = mask_row(start_ref, mask_ref, lane_mask_ref[...], rows)
    for side in range(2):
        base = 2 * side * channels
        pre = dot_nn(turned_weight[base : base + 2 * channels, :], normed)
        gate = jax.nn.sigmoid(pre[channels:])
        coef_ref[0, 2 * side] = (pair_mask * gate).astype(BF16)
        slope = pair_mask * pre[:channels] * gate * (1.0 - gate)
        coef_ref[0, 2 * side + 1] = slope.astype(BF16)
    out_gate = jax.nn.sigmoid(dot_nn(turned_weight[4 * channels :, :], normed))
    upstream = turned(cot_ref[...])
    mixed = (upstream * out_gate).astype(BF16)
    mixed_ref[0] = mixed
    gate_coef_ref[0] = upstream * out_gate * (1.0 - out_gate)
    h = dot_nn(out_weight_ref[...], mixed) * as_column(out_gain_ref[...])
    h = h - jnp.mean(h, axis=0, keepdims=True)
    for row in range(rows):
        h_ref[0, pl.ds(row, channels, stride=rows), :] = h[:, row * LANES : (row + 1) * LANES]


def unpack(recv_ref, base, rows):
    block = recv_ref[:, base : base + 2 * rows, :].astype(F32)
    slabs = block.shape[0]
    return [
        block[:, part * rows : (part + 1) * rows, :].reshape(slabs * rows, LANES).astype(BF16)
        for part in range(2)
    ]


def pack(first, second, slabs):
    rows = first.shape[0] // slabs
    parts = [part.reshape(slabs, rows, LANES) for part in (first, second)]
    return jnp.concatenate(parts, axis=1).astype(BF16)


def slab_unpack_kernel(recv_ref, out_ref):
    slabs = recv_ref.shape[0]
    tokens = out_ref.shape[1]
    rows = tokens // slabs
    for tile in range(tokens // LANES):
        for side in range(2):
            parts = unpack(recv_ref, (tile * 2 + side) * 2 * rows, rows)
            for part in range(2):
                out_ref[side * 2 + part, :, tile * LANES : (tile + 1) * LANES] = parts[part]


def product_kernel(recv_ref, out_ref, slab):
    slabs = recv_ref.shape[0]
    tokens = slab.shape[1]
    slab_unpack_kernel(recv_ref, slab)
    rows = tokens // slabs
    products = [dot_nt(slab[part], slab[2 + part]) for part in range(2)]
    for tile in range(tokens // LANES):
        cols = slice(tile * LANES, (tile + 1) * LANES)
        out_ref[:, tile * 2 * rows : (tile + 1) * 2 * rows, :] = pack(
            products[0][:, cols], products[1][:, cols], slabs
        )


def product_grad_kernel(recv_ref, h_ref, factor_hbm, out_ref, held):
    del factor_hbm
    slabs, group, _ = out_ref.shape
    rows = group // 2
    channels = 2 * slabs
    base = pl.multiple_of(pl.program_id(0) * group, group)
    chunk = 8
    size = 2 * chunk * rows

    def h_at(at):
        return h_ref[0, at * group : at * group + size, :].reshape(2 * chunk, rows, LANES)

    def held_at(at):
        return held[at * group : at * group + size, :].reshape(2 * chunk, rows, LANES)

    total = jnp.zeros((rows, LANES), F32)
    for at in range(0, slabs, chunk):
        block = recv_ref[at : at + chunk, pl.ds(base, group), :].astype(F32)
        held[at * group : at * group + size, :] = block.reshape(size, LANES)
        total = total + jnp.sum(block.reshape(2 * chunk, rows, LANES), axis=0)
    average = (total / channels)[None]
    squares = jnp.zeros((rows, LANES), F32)
    cross = jnp.zeros((rows, LANES), F32)
    for at in range(0, slabs, chunk):
        centered = held_at(at) - average
        squares = squares + jnp.sum(centered * centered, axis=0)
        cross = cross + jnp.sum(centered * h_at(at), axis=0)
    inverse = lax.rsqrt(squares / channels + epsilon)
    slope = inverse * inverse * inverse * (cross / channels)
    inverse, slope = inverse[None], slope[None]
    for at in range(0, slabs, chunk):
        grad = inverse * h_at(at) - (held_at(at) - average) * slope
        out_ref[at : at + chunk] = grad.reshape(chunk, group, LANES).astype(BF16)


def gather_rows(spread, channels, rows):
    return jnp.concatenate(
        [spread[pl.ds(row, channels, stride=rows), :] for row in range(rows)], axis=1
    )


def gate_side_kernel(
    recv_ref, normed_ref, mixed_ref, gate_coef_ref, out_gain_ref, out_bias_ref,
    out_weight_ref, gate_weight_ref,
    gate_normed_ref, share_ref,
    spread, gate_term, out_term, laid,
):
    step = pl.program_id(0)
    channels = normed_ref.shape[1]
    rows = normed_ref.shape[2] // LANES
    group = channels * rows // recv_ref.shape[0]
    block = recv_ref[:, pl.ds(pl.multiple_of(step * group, group), group), :]

    @pl.when(step == 0)
    def _():
        gate_term[...] = jnp.zeros_like(gate_term)
        out_term[...] = jnp.zeros_like(out_term)

    spread[...] = block.astype(F32).reshape(channels * rows, LANES)
    product = gather_rows(spread, channels, rows)
    scaled, _ = norm_columns(product)
    normed_out = (scaled * as_column(out_gain_ref[...]) + as_column(out_bias_ref[...])).astype(BF16)
    projected = dot_tn(out_weight_ref[...], normed_out)
    gate_grad = (projected * gate_coef_ref[0]).astype(BF16)
    gate_normed_ref[0] = dot_nn(gate_weight_ref[...], gate_grad)
    gate_term[...] += dot_nt(normed_ref[0], gate_grad)
    out_term[...] += dot_nt(normed_out, mixed_ref[0])

    @pl.when(step == pl.num_programs(0) - 1)
    def _():
        half = channels // 2
        for which, term in enumerate((gate_term, out_term)):
            for part in range(2):
                value = term[pl.ds(part, half, stride=2), :]
                high = value.astype(BF16).astype(F32)
                laid[pl.ds(part * 4 + which * 2, half, stride=8), :] = high
                laid[pl.ds(part * 4 + which * 2 + 1, half, stride=8), :] = value - high
        share_ref[...] = laid[...].reshape(half, 8, LANES).astype(BF16)


def factor_grad_kernel(
    recv_ref, factor_hbm, early_hbm, out_ref, slab, turned_slab, factor, arrived
):
    del early_hbm
    slabs = recv_ref.shape[0]
    tokens = slab.shape[1]
    rows = tokens // slabs
    loads = [
        pltpu.make_async_copy(factor_hbm.at[which], factor.at[which], arrived.at[which])
        for which in range(4)
    ]
    for which in (2, 3, 0, 1):
        loads[which].start()
    for tile in range(tokens // LANES):
        parts = unpack(recv_ref, tile * 2 * rows, rows)
        for part in range(2):
            slab[part, :, tile * LANES : (tile + 1) * LANES] = parts[part]
    for side in range(2):
        for part in range(2):
            loads[2 * (1 - side) + part].wait()
        if side == 0:
            for part in range(2):
                turned_slab[part] = slab[part].T
        source = slab if side == 0 else turned_slab
        grads = [dot_nn(source[part], factor[2 * (1 - side) + part]) for part in range(2)]
        for tile in range(tokens // LANES):
            cols = slice(tile * LANES, (tile + 1) * LANES)
            base = (tile * 2 + side) * 2 * rows
            out_ref[:, base : base + 2 * rows, :] = pack(
                grads[0][:, cols], grads[1][:, cols], slabs
            )


def proj_blocks(recv_ref, coef_ref, spread, rows):
    step = pl.program_id(0)
    channels = coef_ref.shape[2]
    group = channels * rows // recv_ref.shape[0]
    base = pl.multiple_of(step * 2 * group, 2 * group)
    for side in range(2):
        spread[side] = (
            recv_ref[:, pl.ds(base + side * group, group), :]
            .astype(F32)
            .reshape(channels * rows, LANES)
        )
    blocks = []
    for side in range(2):
        grad = gather_rows(spread.at[side], channels, rows)
        for part in range(2):
            blocks.append((grad * coef_ref[0, 2 * side + part].astype(F32)).astype(BF16))
    return blocks


def proj_grad_kernel(
    recv_ref, coef_ref, normed_ref, early_ref, share_ref, spread, term, laid
):
    step = pl.program_id(0)
    channels = normed_ref.shape[1]
    rows = normed_ref.shape[2] // LANES

    @pl.when(step == 0)
    def _():
        term[...] = jnp.zeros_like(term)

    blocks = proj_blocks(recv_ref, coef_ref, spread, rows)
    for side in range(2):
        both = dot_nt(normed_ref[0], jnp.concatenate(blocks[2 * side : 2 * side + 2], axis=0))
        for part in range(2):
            term[2 * side + part] += both[:, part * channels : (part + 1) * channels]

    @pl.when(step == pl.num_programs(0) - 1)
    def _():
        half = channels // 2
        for part in range(2):
            for block in range(4):
                laid[pl.ds(part * 4 + block, half, stride=8), :] = term[
                    block, pl.ds(part, half, stride=2), :
                ]
        late = laid[...].reshape(half, 8, LANES)
        early = early_ref[...].astype(F32)
        share_ref[...] = jnp.concatenate([late, early], axis=1).astype(BF16)


def pair_grad_kernel(
    recv_ref, coef_ref, gate_normed_ref, x_ref, gain_ref, weight_ref, out_ref, spread
):
    rows = x_ref.shape[0]
    blocks = proj_blocks(recv_ref, coef_ref, spread, rows)
    scaled, inverse = norm_columns(turned(x_ref[...]))
    normed_grad = dot_nn(weight_ref[...], jnp.concatenate(blocks, axis=0)) + gate_normed_ref[0]
    grad = norm_columns_backward(normed_grad * as_column(gain_ref[...]), scaled, inverse)
    for row in range(rows):
        out_ref[row] = grad[:, row * LANES : (row + 1) * LANES].T.astype(BF16)


def weight_sum_kernel(recv_ref, in_ref, out_ref, *, tokens):
    total = jnp.sum(recv_ref[...].astype(F32), axis=0) / tokens
    for part in range(2):
        for block in range(4):
            at = part * 4 + block
            in_ref[part : part + 1, block * LANES : (block + 1) * LANES] = total[at : at + 1]
        at = 8 + part * 4
        in_ref[part : part + 1, 4 * LANES :] = total[at : at + 1] + total[at + 1 : at + 2]
        out_ref[part : part + 1, :] = total[at + 2 : at + 3] + total[at + 3 : at + 4]


def whole(shape):
    return pl.BlockSpec(shape, lambda *_: (0,) * len(shape))


def exchange(values):
    return lax.all_to_all(values, "row", split_axis=0, concat_axis=0, tiled=True)


def params(megabytes):
    return pltpu.CompilerParams(vmem_limit_bytes=megabytes * 1024 * 1024)


def pinned(*arrays):
    return [pltpu.with_memory_space_constraint(array, pltpu.HBM) for array in arrays]


def cost(flops, moved):
    return pl.CostEstimate(flops=flops, bytes_accessed=moved, transcendentals=0)


def on_device(
    pair_state,
    cotangent,
    token_mask,
    input_gain,
    input_bias,
    input_weight,
    output_gain,
    output_bias,
    output_weight,
):
    rows, tokens, channels = pair_state.shape
    slabs = lax.axis_size("row")
    tiles = tokens // LANES
    cells = rows * LANES
    start = (lax.axis_index("row") * rows).astype(jnp.int32).reshape(1)
    lane_mask = token_mask.reshape(1, tokens)
    gain, bias = input_gain.reshape(1, channels), input_bias.reshape(1, channels)
    out_gain, out_bias = output_gain.reshape(1, channels), output_bias.reshape(1, channels)
    smem = pl.BlockSpec(memory_space=pltpu.SMEM)
    lane_spec = pl.BlockSpec((1, LANES), lambda t: (0, t))
    cell_spec = pl.BlockSpec((rows, LANES, channels), lambda t: (0, t, 0))
    row_spec = whole((1, channels))
    column_spec = pl.BlockSpec((1, channels, cells), lambda t: (t, 0, 0))

    def wire_spec(height):
        return pl.BlockSpec((slabs, height, LANES), lambda t: (0, t, 0))

    pair = 2 * rows
    vmem = pl.BlockSpec(memory_space=pltpu.VMEM)
    h_spec = pl.BlockSpec((1, channels * rows, LANES), lambda t: (t, 0, 0))
    coef_spec = pl.BlockSpec((1, 4, channels, cells), lambda t: (t, 0, 0, 0))
    factor_weight_spec = pl.BlockSpec((channels, 4 * channels), lambda t: (0, 0))
    pair_hbm, cot_hbm, lane_hbm, gain, bias, out_gain, out_bias, weight, out_weight = pinned(
        pair_state, cotangent, lane_mask, gain, bias, out_gain, out_bias, input_weight, output_weight
    )

    sent_factors = pl.pallas_call(
        front_kernel,
        name="front",
        grid=(tiles,),
        in_specs=[
            smem, smem, lane_spec, cell_spec, row_spec, row_spec, factor_weight_spec,
        ],
        out_specs=wire_spec(2 * pair),
        out_shape=jax.ShapeDtypeStruct((slabs, 2 * pair * tiles, LANES), BF16),
        scratch_shapes=[
            pltpu.VMEM((4 * channels, channels), BF16),
            pltpu.VMEM((2, channels * rows, LANES), F32),
        ],
        compiler_params=params(16),
        cost_estimate=cost(6 * 10**8, 4 * 10**6),
    )(start, token_mask, lane_hbm, pair_hbm, gain, bias, weight)
    factors = exchange(sent_factors)

    h, coef, normed, mixed, gate_coef = pl.pallas_call(
        side_kernel,
        name="side",
        grid=(tiles,),
        in_specs=[
            smem, smem, lane_spec, cell_spec, cell_spec, row_spec, row_spec,
            whole((channels, 5 * channels)), row_spec, whole((channels, channels)),
        ],
        out_specs=[h_spec, coef_spec, column_spec, column_spec, column_spec],
        out_shape=[
            pltpu.HBM((tiles, channels * rows, LANES), F32),
            pltpu.HBM((tiles, 4, channels, cells), BF16),
            pltpu.HBM((tiles, channels, cells), BF16),
            pltpu.HBM((tiles, channels, cells), BF16),
            pltpu.HBM((tiles, channels, cells), F32),
        ],
        scratch_shapes=[pltpu.VMEM((5 * channels, channels), BF16)],
        compiler_params=params(40),
        cost_estimate=cost(12 * 10**8, 16 * 10**6),
    )(start, token_mask, lane_hbm, pair_hbm, cot_hbm, gain, bias, weight, out_gain, out_weight)
    h, coef, normed, mixed, gate_coef = pinned(h, coef, normed, mixed, gate_coef)

    sent_product = pl.pallas_call(
        product_kernel,
        name="product",
        in_specs=[vmem],
        out_specs=whole((slabs, pair * tiles, LANES)),
        out_shape=pltpu.HBM((slabs, pair * tiles, LANES), BF16),
        scratch_shapes=[pltpu.VMEM((4, tokens, tokens), BF16)],
        compiler_params=params(20),
        cost_estimate=cost(6 * 10**8, 3 * 10**6),
    )(factors)
    product = exchange(sent_product)

    factor_slab = pl.pallas_call(
        slab_unpack_kernel,
        name="slabs",
        in_specs=[vmem],
        out_specs=whole((4, tokens, tokens)),
        out_shape=pltpu.HBM((4, tokens, tokens), BF16),
        compiler_params=params(20),
        cost_estimate=cost(10**6, 4 * 10**6),
    )(factors)
    (factor_slab,) = pinned(factor_slab)

    sent_grad = pl.pallas_call(
        product_grad_kernel,
        name="product_grad",
        grid=(tiles,),
        in_specs=[vmem, h_spec, pl.BlockSpec(memory_space=pl.ANY)],
        out_specs=wire_spec(pair),
        out_shape=pltpu.HBM((slabs, pair * tiles, LANES), BF16),
        scratch_shapes=[pltpu.VMEM((channels * rows, LANES), F32)],
        compiler_params=params(16),
        cost_estimate=cost(10**7, 4 * 10**6),
    )(product, h, factor_slab)
    grad = exchange(sent_grad)

    gate_normed, early_share = pl.pallas_call(
        gate_side_kernel,
        name="gate_side",
        grid=(tiles,),
        in_specs=[
            vmem, column_spec, column_spec, column_spec, row_spec, row_spec,
            whole((channels, channels)),
            pl.BlockSpec((channels, channels), lambda t: (0, 4)),
        ],
        out_specs=[column_spec, whole((slabs, 8, LANES))],
        out_shape=[
            pltpu.HBM((tiles, channels, cells), F32),
            pltpu.HBM((slabs, 8, LANES), BF16),
        ],
        scratch_shapes=[
            pltpu.VMEM((channels * rows, LANES), F32),
            pltpu.VMEM((channels, channels), F32),
            pltpu.VMEM((channels, channels), F32),
            pltpu.VMEM((slabs * 8, LANES), F32),
        ],
        compiler_params=params(24),
        cost_estimate=cost(6 * 10**8, 8 * 10**6),
    )(product, normed, mixed, gate_coef, out_gain, out_bias, out_weight, weight)
    gate_normed, early_share = pinned(gate_normed, early_share)

    height = 2 * pair * tiles
    sent_parts = pl.pallas_call(
        factor_grad_kernel,
        name="factor_grad",
        in_specs=[vmem, pl.BlockSpec(memory_space=pl.ANY), pl.BlockSpec(memory_space=pl.ANY)],
        out_specs=vmem,
        out_shape=jax.ShapeDtypeStruct((slabs, height, LANES), BF16),
        scratch_shapes=[
            pltpu.VMEM((2, tokens, tokens), BF16),
            pltpu.VMEM((2, tokens, tokens), BF16),
            pltpu.VMEM((4, tokens, tokens), BF16),
            pltpu.SemaphoreType.DMA((4,)),
        ],
        compiler_params=params(20),
        cost_estimate=cost(11 * 10**8, 5 * 10**6),
    )(grad, factor_slab, early_share)
    parts = exchange(sent_parts)

    late_share = pl.pallas_call(
        proj_grad_kernel,
        name="proj_grad",
        grid=(tiles,),
        in_specs=[vmem, coef_spec, column_spec, whole((slabs, 8, LANES))],
        out_specs=whole((slabs, 16, LANES)),
        out_shape=pltpu.HBM((slabs, 16, LANES), BF16),
        scratch_shapes=[
            pltpu.VMEM((2, channels * rows, LANES), F32),
            pltpu.VMEM((4, channels, channels), F32),
            pltpu.VMEM((slabs * 8, LANES), F32),
        ],
        compiler_params=params(24),
        cost_estimate=cost(6 * 10**8, 8 * 10**6),
    )(parts, coef, normed, early_share)
    shares = exchange(late_share)

    pair_gradient = pl.pallas_call(
        pair_grad_kernel,
        name="pair_grad",
        grid=(tiles,),
        in_specs=[vmem, coef_spec, column_spec, cell_spec, row_spec, factor_weight_spec],
        out_specs=cell_spec,
        out_shape=pltpu.HBM((rows, tokens, channels), BF16),
        scratch_shapes=[pltpu.VMEM((2, channels * rows, LANES), F32)],
        compiler_params=params(24),
        cost_estimate=cost(6 * 10**8, 8 * 10**6),
    )(parts, coef, gate_normed, pair_hbm, gain, weight)

    held = channels // slabs
    input_gradient, output_gradient = pl.pallas_call(
        lambda *refs: weight_sum_kernel(*refs, tokens=tokens),
        name="weight_sum",
        in_specs=[vmem],
        out_specs=[whole((held, 5 * channels)), whole((held, channels))],
        out_shape=[
            pltpu.HBM((held, 5 * channels), F32),
            pltpu.HBM((held, channels), F32),
        ],
        compiler_params=params(16),
        cost_estimate=cost(10**5, 4 * 10**5),
    )(shares)
    return (pair_gradient, input_gradient, output_gradient)


def solution(mesh):
    return jax.shard_map(
        on_device,
        mesh=mesh,
        in_specs=(
            P(("cplx", "row"), None, None),
            P(("cplx", "row"), None, None),
            P("cplx"),
            P(),
            P(),
            P(),
            P(),
            P(),
            P(),
        ),
        out_specs=(
            P(("cplx", "row"), None, None),
            P(("cplx", "row"), None),
            P(("cplx", "row"), None),
        ),
        check_vma=False,
    )
```

```python
import jax
import jax.numpy as jnp
from jax import lax
from jax.experimental import pallas as pl
from jax.experimental.pallas import tpu as pltpu
from jax.sharding import PartitionSpec as P

epsilon = 1e-05
LANES = 128
F32 = jnp.float32
BF16 = jnp.bfloat16


def dot_nn(a, b):
    return lax.dot_general(a, b, (((1,), (0,)), ((), ())), preferred_element_type=F32)


def dot_nt(a, b):
    return lax.dot_general(a, b, (((1,), (1,)), ((), ())), preferred_element_type=F32)


def dot_tn(a, b):
    return lax.dot_general(a, b, (((0,), (0,)), ((), ())), preferred_element_type=F32)


def eye(size, dtype):
    rows = lax.broadcasted_iota(jnp.int32, (size, size), 0)
    cols = lax.broadcasted_iota(jnp.int32, (size, size), 1)
    return jnp.where(rows == cols, 1.0, 0.0).astype(F32).astype(dtype)


def as_column(row):
    return jnp.sum(eye(row.shape[1], F32) * row, axis=1, keepdims=True)


def turned(block):
    rows, lanes, channels = block.shape
    return dot_nt(eye(channels, BF16), block.reshape(rows * lanes, channels))


def norm_columns(values):
    average = jnp.mean(values, axis=0, keepdims=True)
    centered = values - average
    variance = jnp.mean(centered * centered, axis=0, keepdims=True)
    inverse = lax.rsqrt(variance + epsilon)
    return centered * inverse, inverse


def norm_columns_backward(upstream, scaled, inverse):
    first = jnp.mean(upstream, axis=0, keepdims=True)
    second = jnp.mean(upstream * scaled, axis=0, keepdims=True)
    return inverse * (upstream - first - scaled * second)


def normed_columns(block, gain_row, bias_row):
    scaled, inverse = norm_columns(turned(block))
    normed = (scaled * as_column(gain_row) + as_column(bias_row)).astype(BF16)
    return normed, scaled, inverse


def mask_row(start_ref, mask_ref, lane_mask, rows):
    lane_float = lane_mask.astype(F32)
    parts = [
        lane_float * mask_ref[start_ref[0] + row].astype(F32) for row in range(rows)
    ]
    return jnp.concatenate(parts, axis=1)


def front_kernel(
    start_ref, mask_ref, lane_mask_ref, x_ref, gain_ref, bias_ref, weight_ref, out_ref,
    turned_weight, spread,
):
    rows = x_ref.shape[0]
    channels = x_ref.shape[2]

    @pl.when(pl.program_id(0) == 0)
    def _():
        turned_weight[...] = weight_ref[...].astype(F32).T.astype(BF16)

    gain, bias = as_column(gain_ref[...]), as_column(bias_ref[...])
    lane_mask = lane_mask_ref[...].astype(F32)
    scaled, _ = norm_columns(turned(x_ref[...]))
    normed = (scaled * gain + bias).astype(BF16)
    masks = [lane_mask * mask_ref[start_ref[0] + row].astype(F32) for row in range(rows)]
    pair_mask = jnp.concatenate(masks, axis=1)
    for side in range(2):
        base = 2 * side * channels
        pre = dot_nn(turned_weight[base : base + 2 * channels, :], normed)
        factor = pair_mask * jax.nn.sigmoid(pre[channels:]) * pre[:channels]
        for row in range(rows):
            spread[side, pl.ds(row, channels, stride=rows), :] = factor[
                :, row * LANES : (row + 1) * LANES
            ]
    group = channels * rows // out_ref.shape[0]
    base = pl.multiple_of(pl.program_id(0) * 2 * group, 2 * group)
    for side in range(2):
        out_ref[:, pl.ds(base + side * group, group), :] = (
            spread[side].reshape(out_ref.shape[0], group, LANES).astype(BF16)
        )


def side_kernel(
    start_ref, mask_ref, lane_mask_ref, x_ref, cot_ref, gain_ref, bias_ref, weight_ref,
    out_gain_ref, out_weight_ref,
    h_ref, coef_ref, normed_ref, mixed_ref, gate_coef_ref,
    turned_weight,
):
    rows = x_ref.shape[0]
    channels = x_ref.shape[2]

    @pl.when(pl.program_id(0) == 0)
    def _():
        turned_weight[...] = weight_ref[...].astype(F32).T.astype(BF16)

    normed, _, _ = normed_columns(x_ref[...], gain_ref[...], bias_ref[...])
    normed_ref[0] = normed
    pair_mask = mask_row(start_ref, mask_ref, lane_mask_ref[...], rows)
    for side in range(2):
        base = 2 * side * channels
        pre = dot_nn(turned_weight[base : base + 2 * channels, :], normed)
        gate = jax.nn.sigmoid(pre[channels:])
        coef_ref[0, 2 * side] = (pair_mask * gate).astype(BF16)
        slope = pair_mask * pre[:channels] * gate * (1.0 - gate)
        coef_ref[0, 2 * side + 1] = slope.astype(BF16)
    out_gate = jax.nn.sigmoid(dot_nn(turned_weight[4 * channels :, :], normed))
    upstream = turned(cot_ref[...])
    mixed = (upstream * out_gate).astype(BF16)
    mixed_ref[0] = mixed
    gate_coef_ref[0] = upstream * out_gate * (1.0 - out_gate)
    h = dot_nn(out_weight_ref[...], mixed) * as_column(out_gain_ref[...])
    h = h - jnp.mean(h, axis=0, keepdims=True)
    for row in range(rows):
        h_ref[0, pl.ds(row, channels, stride=rows), :] = h[:, row * LANES : (row + 1) * LANES]


def unpack(recv_ref, base, rows):
    block = recv_ref[:, base : base + 2 * rows, :].astype(F32)
    slabs = block.shape[0]
    return [
        block[:, part * rows : (part + 1) * rows, :].reshape(slabs * rows, LANES).astype(BF16)
        for part in range(2)
    ]


def pack(first, second, slabs):
    rows = first.shape[0] // slabs
    parts = [part.reshape(slabs, rows, LANES) for part in (first, second)]
    return jnp.concatenate(parts, axis=1).astype(BF16)


def slab_unpack_kernel(recv_ref, out_ref):
    slabs = recv_ref.shape[0]
    tokens = out_ref.shape[1]
    rows = tokens // slabs
    for tile in range(tokens // LANES):
        for side in range(2):
            parts = unpack(recv_ref, (tile * 2 + side) * 2 * rows, rows)
            for part in range(2):
                out_ref[side * 2 + part, :, tile * LANES : (tile + 1) * LANES] = parts[part]


def product_kernel(recv_ref, out_ref, slab):
    slabs = recv_ref.shape[0]
    tokens = slab.shape[1]
    slab_unpack_kernel(recv_ref, slab)
    rows = tokens // slabs
    products = [dot_nt(slab[part], slab[2 + part]) for part in range(2)]
    for tile in range(tokens // LANES):
        cols = slice(tile * LANES, (tile + 1) * LANES)
        out_ref[:, tile * 2 * rows : (tile + 1) * 2 * rows, :] = pack(
            products[0][:, cols], products[1][:, cols], slabs
        )


def product_grad_kernel(recv_ref, h_hbm, factor_hbm, out_ref, held, h_ref, arrived):
    del factor_hbm
    step = pl.program_id(0)

    @pl.when(step == 0)
    def _():
        for tile in range(h_hbm.shape[0]):
            pltpu.make_async_copy(h_hbm.at[tile], h_ref.at[tile], arrived.at[tile]).start()

    slabs, group, _ = out_ref.shape
    rows = group // 2
    channels = 2 * slabs
    base = pl.multiple_of(step * group, group)
    chunk = 8
    size = 2 * chunk * rows

    def h_at(at):
        return h_ref[step, at * group : at * group + size, :].reshape(2 * chunk, rows, LANES)

    def held_at(at):
        return held[at * group : at * group + size, :].reshape(2 * chunk, rows, LANES)

    total = jnp.zeros((rows, LANES), F32)
    for at in range(0, slabs, chunk):
        block = recv_ref[at : at + chunk, pl.ds(base, group), :].astype(F32)
        held[at * group : at * group + size, :] = block.reshape(size, LANES)
        total = total + jnp.sum(block.reshape(2 * chunk, rows, LANES), axis=0)
    average = (total / channels)[None]
    pltpu.make_async_copy(h_hbm.at[step], h_ref.at[step], arrived.at[step]).wait()
    squares = jnp.zeros((rows, LANES), F32)
    cross = jnp.zeros((rows, LANES), F32)
    for at in range(0, slabs, chunk):
        centered = held_at(at) - average
        squares = squares + jnp.sum(centered * centered, axis=0)
        cross = cross + jnp.sum(centered * h_at(at), axis=0)
    inverse = lax.rsqrt(squares / channels + epsilon)
    slope = inverse * inverse * inverse * (cross / channels)
    inverse, slope = inverse[None], slope[None]
    for at in range(0, slabs, chunk):
        grad = inverse * h_at(at) - (held_at(at) - average) * slope
        out_ref[at : at + chunk] = grad.reshape(chunk, group, LANES).astype(BF16)


def gather_rows(spread, channels, rows):
    return jnp.concatenate(
        [spread[pl.ds(row, channels, stride=rows), :] for row in range(rows)], axis=1
    )


def gate_side_kernel(
    recv_ref, normed_ref, mixed_ref, gate_coef_ref, out_gain_ref, out_bias_ref,
    out_weight_ref, gate_weight_ref,
    gate_normed_ref, share_ref,
    spread, gate_term, out_term, laid,
):
    step = pl.program_id(0)
    channels = normed_ref.shape[1]
    rows = normed_ref.shape[2] // LANES
    group = channels * rows // recv_ref.shape[0]
    block = recv_ref[:, pl.ds(pl.multiple_of(step * group, group), group), :]

    @pl.when(step == 0)
    def _():
        gate_term[...] = jnp.zeros_like(gate_term)
        out_term[...] = jnp.zeros_like(out_term)

    spread[...] = block.astype(F32).reshape(channels * rows, LANES)
    product = gather_rows(spread, channels, rows)
    scaled, _ = norm_columns(product)
    normed_out = (scaled * as_column(out_gain_ref[...]) + as_column(out_bias_ref[...])).astype(BF16)
    projected = dot_tn(out_weight_ref[...], normed_out)
    gate_grad = (projected * gate_coef_ref[0]).astype(BF16)
    gate_normed_ref[0] = dot_nn(gate_weight_ref[...], gate_grad)
    gate_term[...] += dot_nt(normed_ref[0], gate_grad)
    out_term[...] += dot_nt(normed_out, mixed_ref[0])

    @pl.when(step == pl.num_programs(0) - 1)
    def _():
        half = channels // 2
        for which, term in enumerate((gate_term, out_term)):
            for part in range(2):
                value = term[pl.ds(part, half, stride=2), :]
                high = value.astype(BF16).astype(F32)
                laid[pl.ds(part * 4 + which * 2, half, stride=8), :] = high
                laid[pl.ds(part * 4 + which * 2 + 1, half, stride=8), :] = value - high
        share_ref[...] = laid[...].reshape(half, 8, LANES).astype(BF16)


def factor_grad_kernel(
    recv_ref, factor_hbm, early_hbm, out_ref, slab, turned_slab, factor, arrived
):
    del early_hbm
    slabs = recv_ref.shape[0]
    tokens = slab.shape[1]
    rows = tokens // slabs
    loads = [
        pltpu.make_async_copy(factor_hbm.at[which], factor.at[which], arrived.at[which])
        for which in range(4)
    ]
    for which in (2, 3, 0, 1):
        loads[which].start()
    for tile in range(tokens // LANES):
        parts = unpack(recv_ref, tile * 2 * rows, rows)
        for part in range(2):
            slab[part, :, tile * LANES : (tile + 1) * LANES] = parts[part]
    for side in range(2):
        for part in range(2):
            loads[2 * (1 - side) + part].wait()
        if side == 0:
            for part in range(2):
                turned_slab[part] = slab[part].T
        source = slab if side == 0 else turned_slab
        grads = [dot_nn(source[part], factor[2 * (1 - side) + part]) for part in range(2)]
        for tile in range(tokens // LANES):
            cols = slice(tile * LANES, (tile + 1) * LANES)
            base = (tile * 2 + side) * 2 * rows
            out_ref[:, base : base + 2 * rows, :] = pack(
                grads[0][:, cols], grads[1][:, cols], slabs
            )


def spread_parts(recv_ref, spread, rows):
    step = pl.program_id(0)
    channels = spread.shape[1] // rows
    group = channels * rows // recv_ref.shape[0]
    base = pl.multiple_of(step * 2 * group, 2 * group)
    for side in range(2):
        spread[side] = (
            recv_ref[:, pl.ds(base + side * group, group), :]
            .astype(F32)
            .reshape(channels * rows, LANES)
        )


def proj_blocks(recv_ref, coef_ref, spread, rows):
    channels = coef_ref.shape[2]
    spread_parts(recv_ref, spread, rows)
    blocks = []
    for side in range(2):
        grad = gather_rows(spread.at[side], channels, rows)
        for part in range(2):
            blocks.append((grad * coef_ref[0, 2 * side + part].astype(F32)).astype(BF16))
    return blocks


def proj_grad_kernel(
    recv_ref, coef_ref, normed_ref, early_ref, share_ref, spread, term, laid
):
    step = pl.program_id(0)
    channels = normed_ref.shape[1]
    rows = normed_ref.shape[2] // LANES

    @pl.when(step == 0)
    def _():
        term[...] = jnp.zeros_like(term)

    spread_parts(recv_ref, spread, rows)
    for side in range(2):
        both = None
        for row in range(0, rows, 4):
            cols = slice(row * LANES, (row + 4) * LANES)
            grad = jnp.concatenate(
                [spread[side, pl.ds(at, channels, stride=rows), :] for at in range(row, row + 4)],
                axis=1,
            )
            values = [
                (grad * coef_ref[0, 2 * side + part, :, cols].astype(F32)).astype(BF16)
                for part in range(2)
            ]
            piece = dot_nt(normed_ref[0, :, cols], jnp.concatenate(values, axis=0))
            both = piece if both is None else both + piece
        for part in range(2):
            term[2 * side + part] += both[:, part * channels : (part + 1) * channels]

    @pl.when(step == pl.num_programs(0) - 1)
    def _():
        half = channels // 2
        for part in range(2):
            for block in range(4):
                laid[pl.ds(part * 4 + block, half, stride=8), :] = term[
                    block, pl.ds(part, half, stride=2), :
                ]
        late = laid[...].reshape(half, 8, LANES)
        early = early_ref[...].astype(F32)
        share_ref[...] = jnp.concatenate([late, early], axis=1).astype(BF16)


def pair_grad_kernel(
    recv_ref, coef_ref, gate_normed_ref, x_ref, gain_ref, weight_ref, out_ref, spread
):
    rows = x_ref.shape[0]
    blocks = proj_blocks(recv_ref, coef_ref, spread, rows)
    scaled, inverse = norm_columns(turned(x_ref[...]))
    normed_grad = dot_nn(weight_ref[...], jnp.concatenate(blocks, axis=0)) + gate_normed_ref[0]
    grad = norm_columns_backward(normed_grad * as_column(gain_ref[...]), scaled, inverse)
    for row in range(rows):
        out_ref[row] = grad[:, row * LANES : (row + 1) * LANES].T.astype(BF16)


def weight_sum_kernel(recv_ref, in_ref, out_ref, *, tokens):
    total = jnp.sum(recv_ref[...].astype(F32), axis=0) / tokens
    for part in range(2):
        for block in range(4):
            at = part * 4 + block
            in_ref[part : part + 1, block * LANES : (block + 1) * LANES] = total[at : at + 1]
        at = 8 + part * 4
        in_ref[part : part + 1, 4 * LANES :] = total[at : at + 1] + total[at + 1 : at + 2]
        out_ref[part : part + 1, :] = total[at + 2 : at + 3] + total[at + 3 : at + 4]


def whole(shape):
    return pl.BlockSpec(shape, lambda *_: (0,) * len(shape))


def exchange(values):
    return lax.all_to_all(values, "row", split_axis=0, concat_axis=0, tiled=True)


def params(megabytes):
    return pltpu.CompilerParams(vmem_limit_bytes=megabytes * 1024 * 1024)


def pinned(*arrays):
    return [pltpu.with_memory_space_constraint(array, pltpu.HBM) for array in arrays]


def cost(flops, moved):
    return pl.CostEstimate(flops=flops, bytes_accessed=moved, transcendentals=0)


def on_device(
    pair_state,
    cotangent,
    token_mask,
    input_gain,
    input_bias,
    input_weight,
    output_gain,
    output_bias,
    output_weight,
):
    rows, tokens, channels = pair_state.shape
    slabs = lax.axis_size("row")
    tiles = tokens // LANES
    cells = rows * LANES
    start = (lax.axis_index("row") * rows).astype(jnp.int32).reshape(1)
    lane_mask = token_mask.reshape(1, tokens)
    gain, bias = input_gain.reshape(1, channels), input_bias.reshape(1, channels)
    out_gain, out_bias = output_gain.reshape(1, channels), output_bias.reshape(1, channels)
    smem = pl.BlockSpec(memory_space=pltpu.SMEM)
    lane_spec = pl.BlockSpec((1, LANES), lambda t: (0, t))
    cell_spec = pl.BlockSpec((rows, LANES, channels), lambda t: (0, t, 0))
    row_spec = whole((1, channels))
    column_spec = pl.BlockSpec((1, channels, cells), lambda t: (t, 0, 0))

    def wire_spec(height):
        return pl.BlockSpec((slabs, height, LANES), lambda t: (0, t, 0))

    pair = 2 * rows
    vmem = pl.BlockSpec(memory_space=pltpu.VMEM)
    anywhere = pl.BlockSpec(memory_space=pl.ANY)
    h_spec = pl.BlockSpec((1, channels * rows, LANES), lambda t: (t, 0, 0))
    coef_spec = pl.BlockSpec((1, 4, channels, cells), lambda t: (t, 0, 0, 0))
    factor_weight_spec = pl.BlockSpec((channels, 4 * channels), lambda t: (0, 0))
    pair_hbm, cot_hbm, lane_hbm, gain, bias, out_gain, out_bias, weight, out_weight = pinned(
        pair_state, cotangent, lane_mask, gain, bias, out_gain, out_bias, input_weight, output_weight
    )

    sent_factors = pl.pallas_call(
        front_kernel,
        name="front",
        grid=(tiles,),
        in_specs=[
            smem, smem, lane_spec, cell_spec, row_spec, row_spec, factor_weight_spec,
        ],
        out_specs=vmem,
        out_shape=jax.ShapeDtypeStruct((slabs, 2 * pair * tiles, LANES), BF16),
        scratch_shapes=[
            pltpu.VMEM((4 * channels, channels), BF16),
            pltpu.VMEM((2, channels * rows, LANES), F32),
        ],
        compiler_params=params(16),
        cost_estimate=cost(6 * 10**8, 4 * 10**6),
    )(start, token_mask, lane_hbm, pair_hbm, gain, bias, weight)
    factors = exchange(sent_factors)

    h, coef, normed, mixed, gate_coef = pl.pallas_call(
        side_kernel,
        name="side",
        grid=(tiles,),
        in_specs=[
            smem, smem, lane_spec, cell_spec, cell_spec, row_spec, row_spec,
            whole((channels, 5 * channels)), row_spec, whole((channels, channels)),
        ],
        out_specs=[h_spec, coef_spec, column_spec, column_spec, column_spec],
        out_shape=[
            pltpu.HBM((tiles, channels * rows, LANES), F32),
            pltpu.HBM((tiles, 4, channels, cells), BF16),
            pltpu.HBM((tiles, channels, cells), BF16),
            pltpu.HBM((tiles, channels, cells), BF16),
            pltpu.HBM((tiles, channels, cells), F32),
        ],
        scratch_shapes=[pltpu.VMEM((5 * channels, channels), BF16)],
        compiler_params=params(40),
        cost_estimate=cost(12 * 10**8, 16 * 10**6),
    )(start, token_mask, lane_hbm, pair_hbm, cot_hbm, gain, bias, weight, out_gain, out_weight)
    h, coef, normed, mixed, gate_coef = pinned(h, coef, normed, mixed, gate_coef)

    sent_product = pl.pallas_call(
        product_kernel,
        name="product",
        in_specs=[vmem],
        out_specs=whole((slabs, pair * tiles, LANES)),
        out_shape=pltpu.HBM((slabs, pair * tiles, LANES), BF16),
        scratch_shapes=[pltpu.VMEM((4, tokens, tokens), BF16)],
        compiler_params=params(20),
        cost_estimate=cost(6 * 10**8, 3 * 10**6),
    )(factors)
    product = exchange(sent_product)

    factor_slab = pl.pallas_call(
        slab_unpack_kernel,
        name="slabs",
        in_specs=[vmem],
        out_specs=whole((4, tokens, tokens)),
        out_shape=pltpu.HBM((4, tokens, tokens), BF16),
        compiler_params=params(20),
        cost_estimate=cost(10**6, 4 * 10**6),
    )(factors)
    (factor_slab,) = pinned(factor_slab)

    sent_grad = pl.pallas_call(
        product_grad_kernel,
        name="product_grad",
        grid=(tiles,),
        in_specs=[vmem, anywhere, anywhere],
        out_specs=wire_spec(pair),
        out_shape=pltpu.HBM((slabs, pair * tiles, LANES), BF16),
        scratch_shapes=[
            pltpu.VMEM((channels * rows, LANES), F32),
            pltpu.VMEM((tiles, channels * rows, LANES), F32),
            pltpu.SemaphoreType.DMA((tiles,)),
        ],
        compiler_params=params(16),
        cost_estimate=cost(10**7, 4 * 10**6),
    )(product, h, factor_slab)
    grad = exchange(sent_grad)

    gate_normed, early_share = pl.pallas_call(
        gate_side_kernel,
        name="gate_side",
        grid=(tiles,),
        in_specs=[
            vmem, column_spec, column_spec, column_spec, row_spec, row_spec,
            whole((channels, channels)),
            pl.BlockSpec((channels, channels), lambda t: (0, 4)),
        ],
        out_specs=[column_spec, whole((slabs, 8, LANES))],
        out_shape=[
            pltpu.HBM((tiles, channels, cells), F32),
            pltpu.HBM((slabs, 8, LANES), BF16),
        ],
        scratch_shapes=[
            pltpu.VMEM((channels * rows, LANES), F32),
            pltpu.VMEM((channels, channels), F32),
            pltpu.VMEM((channels, channels), F32),
            pltpu.VMEM((slabs * 8, LANES), F32),
        ],
        compiler_params=params(24),
        cost_estimate=cost(6 * 10**8, 8 * 10**6),
    )(product, normed, mixed, gate_coef, out_gain, out_bias, out_weight, weight)
    gate_normed, early_share = pinned(gate_normed, early_share)

    height = 2 * pair * tiles
    sent_parts = pl.pallas_call(
        factor_grad_kernel,
        name="factor_grad",
        in_specs=[vmem, anywhere, anywhere],
        out_specs=vmem,
        out_shape=jax.ShapeDtypeStruct((slabs, height, LANES), BF16),
        scratch_shapes=[
            pltpu.VMEM((2, tokens, tokens), BF16),
            pltpu.VMEM((2, tokens, tokens), BF16),
            pltpu.VMEM((4, tokens, tokens), BF16),
            pltpu.SemaphoreType.DMA((4,)),
        ],
        compiler_params=params(20),
        cost_estimate=cost(11 * 10**8, 5 * 10**6),
    )(grad, factor_slab, early_share)
    parts = exchange(sent_parts)

    late_share = pl.pallas_call(
        proj_grad_kernel,
        name="proj_grad",
        grid=(tiles,),
        in_specs=[vmem, coef_spec, column_spec, whole((slabs, 8, LANES))],
        out_specs=whole((slabs, 16, LANES)),
        out_shape=pltpu.HBM((slabs, 16, LANES), BF16),
        scratch_shapes=[
            pltpu.VMEM((2, channels * rows, LANES), F32),
            pltpu.VMEM((4, channels, channels), F32),
            pltpu.VMEM((slabs * 8, LANES), F32),
        ],
        compiler_params=params(24),
        cost_estimate=cost(6 * 10**8, 8 * 10**6),
    )(parts, coef, normed, early_share)
    shares = exchange(late_share)

    pair_gradient = pl.pallas_call(
        pair_grad_kernel,
        name="pair_grad",
        grid=(tiles,),
        in_specs=[vmem, coef_spec, column_spec, cell_spec, row_spec, factor_weight_spec],
        out_specs=cell_spec,
        out_shape=pltpu.HBM((rows, tokens, channels), BF16),
        scratch_shapes=[pltpu.VMEM((2, channels * rows, LANES), F32)],
        compiler_params=params(24),
        cost_estimate=cost(6 * 10**8, 8 * 10**6),
    )(parts, coef, gate_normed, pair_hbm, gain, weight)

    held = channels // slabs
    input_gradient, output_gradient = pl.pallas_call(
        lambda *refs: weight_sum_kernel(*refs, tokens=tokens),
        name="weight_sum",
        in_specs=[vmem],
        out_specs=[whole((held, 5 * channels)), whole((held, channels))],
        out_shape=[
            pltpu.HBM((held, 5 * channels), F32),
            pltpu.HBM((held, channels), F32),
        ],
        compiler_params=params(16),
        cost_estimate=cost(10**5, 4 * 10**5),
    )(shares)
    return (pair_gradient, input_gradient, output_gradient)


def solution(mesh):
    return jax.shard_map(
        on_device,
        mesh=mesh,
        in_specs=(
            P(("cplx", "row"), None, None),
            P(("cplx", "row"), None, None),
            P("cplx"),
            P(),
            P(),
            P(),
            P(),
            P(),
            P(),
        ),
        out_specs=(
            P(("cplx", "row"), None, None),
            P(("cplx", "row"), None),
            P(("cplx", "row"), None),
        ),
        check_vma=False,
    )
```

```python
import jax
import jax.numpy as jnp
from jax import lax
from jax.experimental import pallas as pl
from jax.experimental.pallas import tpu as pltpu
from jax.sharding import PartitionSpec as P

epsilon = 1e-05
LANES = 128
F32 = jnp.float32
BF16 = jnp.bfloat16


def dot_nn(a, b):
    return lax.dot_general(a, b, (((1,), (0,)), ((), ())), preferred_element_type=F32)


def dot_nt(a, b):
    return lax.dot_general(a, b, (((1,), (1,)), ((), ())), preferred_element_type=F32)


def dot_tn(a, b):
    return lax.dot_general(a, b, (((0,), (0,)), ((), ())), preferred_element_type=F32)


def eye(size, dtype):
    rows = lax.broadcasted_iota(jnp.int32, (size, size), 0)
    cols = lax.broadcasted_iota(jnp.int32, (size, size), 1)
    return jnp.where(rows == cols, 1.0, 0.0).astype(F32).astype(dtype)


def as_column(row):
    return jnp.sum(eye(row.shape[1], F32) * row, axis=1, keepdims=True)


def turned(block):
    rows, lanes, channels = block.shape
    return dot_nt(eye(channels, BF16), block.reshape(rows * lanes, channels))


def norm_columns(values):
    average = jnp.mean(values, axis=0, keepdims=True)
    centered = values - average
    variance = jnp.mean(centered * centered, axis=0, keepdims=True)
    inverse = lax.rsqrt(variance + epsilon)
    return centered * inverse, inverse


def norm_columns_backward(upstream, scaled, inverse):
    first = jnp.mean(upstream, axis=0, keepdims=True)
    second = jnp.mean(upstream * scaled, axis=0, keepdims=True)
    return inverse * (upstream - first - scaled * second)


def normed_columns(block, gain_row, bias_row):
    scaled, inverse = norm_columns(turned(block))
    normed = (scaled * as_column(gain_row) + as_column(bias_row)).astype(BF16)
    return normed, scaled, inverse


def mask_row(start_ref, mask_ref, lane_mask, rows):
    lane_float = lane_mask.astype(F32)
    parts = [
        lane_float * mask_ref[start_ref[0] + row].astype(F32) for row in range(rows)
    ]
    return jnp.concatenate(parts, axis=1)


def front_kernel(
    start_ref, mask_ref, lane_mask_ref, x_ref, gain_ref, bias_ref, weight_ref, out_ref,
    turned_weight, spread,
):
    rows = x_ref.shape[0]
    channels = x_ref.shape[2]

    @pl.when(pl.program_id(0) == 0)
    def _():
        turned_weight[...] = weight_ref[...].astype(F32).T.astype(BF16)

    gain, bias = as_column(gain_ref[...]), as_column(bias_ref[...])
    lane_mask = lane_mask_ref[...].astype(F32)
    scaled, _ = norm_columns(turned(x_ref[...]))
    normed = (scaled * gain + bias).astype(BF16)
    masks = [lane_mask * mask_ref[start_ref[0] + row].astype(F32) for row in range(rows)]
    pair_mask = jnp.concatenate(masks, axis=1)
    for side in range(2):
        base = 2 * side * channels
        pre = dot_nn(turned_weight[base : base + 2 * channels, :], normed)
        factor = pair_mask * jax.nn.sigmoid(pre[channels:]) * pre[:channels]
        for row in range(rows):
            spread[side, pl.ds(row, channels, stride=rows), :] = factor[
                :, row * LANES : (row + 1) * LANES
            ]
    group = channels * rows // out_ref.shape[0]
    base = pl.multiple_of(pl.program_id(0) * 2 * group, 2 * group)
    for side in range(2):
        out_ref[:, pl.ds(base + side * group, group), :] = (
            spread[side].reshape(out_ref.shape[0], group, LANES).astype(BF16)
        )


def side_kernel(
    start_ref, mask_ref, lane_mask_ref, x_ref, cot_ref, gain_ref, bias_ref, weight_ref,
    out_gain_ref, out_weight_ref,
    h_ref, coef_ref, normed_ref, mixed_ref, gate_coef_ref,
    turned_weight,
):
    rows = x_ref.shape[0]
    channels = x_ref.shape[2]

    @pl.when(pl.program_id(0) == 0)
    def _():
        turned_weight[...] = weight_ref[...].astype(F32).T.astype(BF16)

    normed, _, _ = normed_columns(x_ref[...], gain_ref[...], bias_ref[...])
    normed_ref[0] = normed
    pair_mask = mask_row(start_ref, mask_ref, lane_mask_ref[...], rows)
    for side in range(2):
        base = 2 * side * channels
        pre = dot_nn(turned_weight[base : base + 2 * channels, :], normed)
        gate = jax.nn.sigmoid(pre[channels:])
        coef_ref[0, 2 * side] = (pair_mask * gate).astype(BF16)
        slope = pair_mask * pre[:channels] * gate * (1.0 - gate)
        coef_ref[0, 2 * side + 1] = slope.astype(BF16)
    out_gate = jax.nn.sigmoid(dot_nn(turned_weight[4 * channels :, :], normed))
    upstream = turned(cot_ref[...])
    mixed = (upstream * out_gate).astype(BF16)
    mixed_ref[0] = mixed
    gate_coef_ref[0] = upstream * out_gate * (1.0 - out_gate)
    h = dot_nn(out_weight_ref[...], mixed) * as_column(out_gain_ref[...])
    h = h - jnp.mean(h, axis=0, keepdims=True)
    for row in range(rows):
        h_ref[0, pl.ds(row, channels, stride=rows), :] = h[:, row * LANES : (row + 1) * LANES]


def unpack(recv_ref, base, rows):
    block = recv_ref[:, base : base + 2 * rows, :].astype(F32)
    slabs = block.shape[0]
    return [
        block[:, part * rows : (part + 1) * rows, :].reshape(slabs * rows, LANES).astype(BF16)
        for part in range(2)
    ]


def pack(first, second, slabs):
    rows = first.shape[0] // slabs
    parts = [part.reshape(slabs, rows, LANES) for part in (first, second)]
    return jnp.concatenate(parts, axis=1).astype(BF16)


def slab_unpack_kernel(recv_ref, out_ref):
    slabs = recv_ref.shape[0]
    tokens = out_ref.shape[1]
    rows = tokens // slabs
    for tile in range(tokens // LANES):
        for side in range(2):
            parts = unpack(recv_ref, (tile * 2 + side) * 2 * rows, rows)
            for part in range(2):
                out_ref[side * 2 + part, :, tile * LANES : (tile + 1) * LANES] = parts[part]


def product_kernel(recv_ref, out_ref, slab):
    slabs = recv_ref.shape[0]
    tokens = slab.shape[1]
    slab_unpack_kernel(recv_ref, slab)
    rows = tokens // slabs
    products = [dot_nt(slab[part], slab[2 + part]) for part in range(2)]
    for tile in range(tokens // LANES):
        cols = slice(tile * LANES, (tile + 1) * LANES)
        out_ref[:, tile * 2 * rows : (tile + 1) * 2 * rows, :] = pack(
            products[0][:, cols], products[1][:, cols], slabs
        )


def product_grad_kernel(recv_ref, h_hbm, factor_hbm, out_ref, held, h_ref, arrived):
    del factor_hbm
    step = pl.program_id(0)

    @pl.when(step == 0)
    def _():
        for tile in range(h_hbm.shape[0]):
            pltpu.make_async_copy(h_hbm.at[tile], h_ref.at[tile], arrived.at[tile]).start()

    slabs, group, _ = out_ref.shape
    rows = group // 2
    channels = 2 * slabs
    base = pl.multiple_of(step * group, group)
    chunk = 8
    size = 2 * chunk * rows

    def h_at(at):
        return h_ref[step, at * group : at * group + size, :].reshape(2 * chunk, rows, LANES)

    def held_at(at):
        return held[at * group : at * group + size, :].reshape(2 * chunk, rows, LANES)

    total = jnp.zeros((rows, LANES), F32)
    for at in range(0, slabs, chunk):
        block = recv_ref[at : at + chunk, pl.ds(base, group), :].astype(F32)
        held[at * group : at * group + size, :] = block.reshape(size, LANES)
        total = total + jnp.sum(block.reshape(2 * chunk, rows, LANES), axis=0)
    average = (total / channels)[None]
    pltpu.make_async_copy(h_hbm.at[step], h_ref.at[step], arrived.at[step]).wait()
    squares = jnp.zeros((rows, LANES), F32)
    cross = jnp.zeros((rows, LANES), F32)
    for at in range(0, slabs, chunk):
        centered = held_at(at) - average
        squares = squares + jnp.sum(centered * centered, axis=0)
        cross = cross + jnp.sum(centered * h_at(at), axis=0)
    inverse = lax.rsqrt(squares / channels + epsilon)
    slope = inverse * inverse * inverse * (cross / channels)
    inverse, slope = inverse[None], slope[None]
    for at in range(0, slabs, chunk):
        grad = inverse * h_at(at) - (held_at(at) - average) * slope
        out_ref[at : at + chunk] = grad.reshape(chunk, group, LANES).astype(BF16)


def gather_rows(spread, channels, rows):
    return jnp.concatenate(
        [spread[pl.ds(row, channels, stride=rows), :] for row in range(rows)], axis=1
    )


def gate_side_kernel(
    recv_ref, normed_ref, mixed_ref, gate_coef_ref, out_gain_ref, out_bias_ref,
    out_weight_ref, gate_weight_ref,
    gate_normed_ref, share_ref,
    spread, gate_term, out_term, laid,
):
    step = pl.program_id(0)
    channels = normed_ref.shape[1]
    rows = normed_ref.shape[2] // LANES
    group = channels * rows // recv_ref.shape[0]
    block = recv_ref[:, pl.ds(pl.multiple_of(step * group, group), group), :]

    @pl.when(step == 0)
    def _():
        gate_term[...] = jnp.zeros_like(gate_term)
        out_term[...] = jnp.zeros_like(out_term)

    spread[...] = block.astype(F32).reshape(channels * rows, LANES)
    product = gather_rows(spread, channels, rows)
    scaled, _ = norm_columns(product)
    normed_out = (scaled * as_column(out_gain_ref[...]) + as_column(out_bias_ref[...])).astype(BF16)
    projected = dot_tn(out_weight_ref[...], normed_out)
    gate_grad = (projected * gate_coef_ref[0]).astype(BF16)
    gate_normed_ref[0] = dot_nn(gate_weight_ref[...], gate_grad)
    gate_term[...] += dot_nt(normed_ref[0], gate_grad)
    out_term[...] += dot_nt(normed_out, mixed_ref[0])

    @pl.when(step == pl.num_programs(0) - 1)
    def _():
        half = channels // 2
        for which, term in enumerate((gate_term, out_term)):
            for part in range(2):
                value = term[pl.ds(part, half, stride=2), :]
                high = value.astype(BF16).astype(F32)
                laid[pl.ds(part * 4 + which * 2, half, stride=8), :] = high
                laid[pl.ds(part * 4 + which * 2 + 1, half, stride=8), :] = value - high
        share_ref[...] = laid[...].reshape(half, 8, LANES).astype(BF16)


def factor_grad_kernel(
    recv_ref, factor_hbm, early_hbm, out_ref, slab, turned_slab, factor, arrived
):
    del early_hbm
    slabs = recv_ref.shape[0]
    tokens = slab.shape[1]
    rows = tokens // slabs
    loads = [
        pltpu.make_async_copy(factor_hbm.at[which], factor.at[which], arrived.at[which])
        for which in range(4)
    ]
    for which in (2, 3, 0, 1):
        loads[which].start()
    for tile in range(tokens // LANES):
        parts = unpack(recv_ref, tile * 2 * rows, rows)
        for part in range(2):
            slab[part, :, tile * LANES : (tile + 1) * LANES] = parts[part]
    for side in range(2):
        for part in range(2):
            loads[2 * (1 - side) + part].wait()
        if side == 0:
            for part in range(2):
                turned_slab[part] = slab[part].T
        source = slab if side == 0 else turned_slab
        grads = [dot_nn(source[part], factor[2 * (1 - side) + part]) for part in range(2)]
        for tile in range(tokens // LANES):
            cols = slice(tile * LANES, (tile + 1) * LANES)
            base = (tile * 2 + side) * 2 * rows
            out_ref[:, base : base + 2 * rows, :] = pack(
                grads[0][:, cols], grads[1][:, cols], slabs
            )


def spread_parts(recv_ref, spread, rows):
    step = pl.program_id(0)
    channels = spread.shape[1] // rows
    group = channels * rows // recv_ref.shape[0]
    base = pl.multiple_of(step * 2 * group, 2 * group)
    for side in range(2):
        spread[side] = (
            recv_ref[:, pl.ds(base + side * group, group), :]
            .astype(F32)
            .reshape(channels * rows, LANES)
        )


def proj_blocks(recv_ref, coef_ref, spread, rows):
    channels = coef_ref.shape[2]
    spread_parts(recv_ref, spread, rows)
    blocks = []
    for side in range(2):
        grad = gather_rows(spread.at[side], channels, rows).astype(BF16)
        for part in range(2):
            blocks.append(grad * coef_ref[0, 2 * side + part])
    return blocks


def proj_grad_kernel(
    recv_ref, coef_ref, normed_ref, early_ref, share_ref, spread, term, laid
):
    step = pl.program_id(0)
    channels = normed_ref.shape[1]
    rows = normed_ref.shape[2] // LANES

    @pl.when(step == 0)
    def _():
        term[...] = jnp.zeros_like(term)

    spread_parts(recv_ref, spread, rows)
    for side in range(2):
        both = None
        for row in range(0, rows, 4):
            cols = slice(row * LANES, (row + 4) * LANES)
            grad = jnp.concatenate(
                [spread[side, pl.ds(at, channels, stride=rows), :] for at in range(row, row + 4)],
                axis=1,
            )
            grad = grad.astype(BF16)
            values = [grad * coef_ref[0, 2 * side + part, :, cols] for part in range(2)]
            piece = dot_nt(normed_ref[0, :, cols], jnp.concatenate(values, axis=0))
            both = piece if both is None else both + piece
        for part in range(2):
            term[2 * side + part] += both[:, part * channels : (part + 1) * channels]

    @pl.when(step == pl.num_programs(0) - 1)
    def _():
        half = channels // 2
        for part in range(2):
            for block in range(4):
                laid[pl.ds(part * 4 + block, half, stride=8), :] = term[
                    block, pl.ds(part, half, stride=2), :
                ]
        late = laid[...].reshape(half, 8, LANES)
        early = early_ref[...].astype(F32)
        share_ref[...] = jnp.concatenate([late, early], axis=1).astype(BF16)


def pair_grad_kernel(
    recv_ref, coef_ref, gate_normed_ref, x_ref, gain_ref, weight_ref, out_ref, spread
):
    rows = x_ref.shape[0]
    blocks = proj_blocks(recv_ref, coef_ref, spread, rows)
    scaled, inverse = norm_columns(turned(x_ref[...]))
    normed_grad = dot_nn(weight_ref[...], jnp.concatenate(blocks, axis=0)) + gate_normed_ref[0]
    grad = norm_columns_backward(normed_grad * as_column(gain_ref[...]), scaled, inverse)
    for row in range(rows):
        out_ref[row] = grad[:, row * LANES : (row + 1) * LANES].T.astype(BF16)


def weight_sum_kernel(recv_ref, in_ref, out_ref, *, tokens):
    total = jnp.sum(recv_ref[...].astype(F32), axis=0) / tokens
    for part in range(2):
        for block in range(4):
            at = part * 4 + block
            in_ref[part : part + 1, block * LANES : (block + 1) * LANES] = total[at : at + 1]
        at = 8 + part * 4
        in_ref[part : part + 1, 4 * LANES :] = total[at : at + 1] + total[at + 1 : at + 2]
        out_ref[part : part + 1, :] = total[at + 2 : at + 3] + total[at + 3 : at + 4]


def whole(shape):
    return pl.BlockSpec(shape, lambda *_: (0,) * len(shape))


def exchange(values):
    return lax.all_to_all(values, "row", split_axis=0, concat_axis=0, tiled=True)


def params(megabytes):
    return pltpu.CompilerParams(vmem_limit_bytes=megabytes * 1024 * 1024)


def pinned(*arrays):
    return [pltpu.with_memory_space_constraint(array, pltpu.HBM) for array in arrays]


def cost(flops, moved):
    return pl.CostEstimate(flops=flops, bytes_accessed=moved, transcendentals=0)


def on_device(
    pair_state,
    cotangent,
    token_mask,
    input_gain,
    input_bias,
    input_weight,
    output_gain,
    output_bias,
    output_weight,
):
    rows, tokens, channels = pair_state.shape
    slabs = lax.axis_size("row")
    tiles = tokens // LANES
    cells = rows * LANES
    start = (lax.axis_index("row") * rows).astype(jnp.int32).reshape(1)
    lane_mask = token_mask.reshape(1, tokens)
    gain, bias = input_gain.reshape(1, channels), input_bias.reshape(1, channels)
    out_gain, out_bias = output_gain.reshape(1, channels), output_bias.reshape(1, channels)
    smem = pl.BlockSpec(memory_space=pltpu.SMEM)
    lane_spec = pl.BlockSpec((1, LANES), lambda t: (0, t))
    cell_spec = pl.BlockSpec((rows, LANES, channels), lambda t: (0, t, 0))
    row_spec = whole((1, channels))
    column_spec = pl.BlockSpec((1, channels, cells), lambda t: (t, 0, 0))

    def wire_spec(height):
        return pl.BlockSpec((slabs, height, LANES), lambda t: (0, t, 0))

    pair = 2 * rows
    vmem = pl.BlockSpec(memory_space=pltpu.VMEM)
    anywhere = pl.BlockSpec(memory_space=pl.ANY)
    h_spec = pl.BlockSpec((1, channels * rows, LANES), lambda t: (t, 0, 0))
    coef_spec = pl.BlockSpec((1, 4, channels, cells), lambda t: (t, 0, 0, 0))
    factor_weight_spec = pl.BlockSpec((channels, 4 * channels), lambda t: (0, 0))
    pair_hbm, cot_hbm, lane_hbm, gain, bias, out_gain, out_bias, weight, out_weight = pinned(
        pair_state, cotangent, lane_mask, gain, bias, out_gain, out_bias, input_weight, output_weight
    )

    sent_factors = pl.pallas_call(
        front_kernel,
        name="front",
        grid=(tiles,),
        in_specs=[
            smem, smem, lane_spec, cell_spec, row_spec, row_spec, factor_weight_spec,
        ],
        out_specs=vmem,
        out_shape=jax.ShapeDtypeStruct((slabs, 2 * pair * tiles, LANES), BF16),
        scratch_shapes=[
            pltpu.VMEM((4 * channels, channels), BF16),
            pltpu.VMEM((2, channels * rows, LANES), F32),
        ],
        compiler_params=params(16),
        cost_estimate=cost(6 * 10**8, 4 * 10**6),
    )(start, token_mask, lane_hbm, pair_hbm, gain, bias, weight)
    factors = exchange(sent_factors)

    h, coef, normed, mixed, gate_coef = pl.pallas_call(
        side_kernel,
        name="side",
        grid=(tiles,),
        in_specs=[
            smem, smem, lane_spec, cell_spec, cell_spec, row_spec, row_spec,
            whole((channels, 5 * channels)), row_spec, whole((channels, channels)),
        ],
        out_specs=[h_spec, coef_spec, column_spec, column_spec, column_spec],
        out_shape=[
            pltpu.HBM((tiles, channels * rows, LANES), F32),
            pltpu.HBM((tiles, 4, channels, cells), BF16),
            pltpu.HBM((tiles, channels, cells), BF16),
            pltpu.HBM((tiles, channels, cells), BF16),
            pltpu.HBM((tiles, channels, cells), F32),
        ],
        scratch_shapes=[pltpu.VMEM((5 * channels, channels), BF16)],
        compiler_params=params(40),
        cost_estimate=cost(12 * 10**8, 16 * 10**6),
    )(start, token_mask, lane_hbm, pair_hbm, cot_hbm, gain, bias, weight, out_gain, out_weight)
    h, coef, normed, mixed, gate_coef = pinned(h, coef, normed, mixed, gate_coef)

    sent_product = pl.pallas_call(
        product_kernel,
        name="product",
        in_specs=[vmem],
        out_specs=whole((slabs, pair * tiles, LANES)),
        out_shape=pltpu.HBM((slabs, pair * tiles, LANES), BF16),
        scratch_shapes=[pltpu.VMEM((4, tokens, tokens), BF16)],
        compiler_params=params(20),
        cost_estimate=cost(6 * 10**8, 3 * 10**6),
    )(factors)
    product = exchange(sent_product)

    factor_slab = pl.pallas_call(
        slab_unpack_kernel,
        name="slabs",
        in_specs=[vmem],
        out_specs=whole((4, tokens, tokens)),
        out_shape=pltpu.HBM((4, tokens, tokens), BF16),
        compiler_params=params(20),
        cost_estimate=cost(10**6, 4 * 10**6),
    )(factors)
    (factor_slab,) = pinned(factor_slab)

    sent_grad = pl.pallas_call(
        product_grad_kernel,
        name="product_grad",
        grid=(tiles,),
        in_specs=[vmem, anywhere, anywhere],
        out_specs=wire_spec(pair),
        out_shape=pltpu.HBM((slabs, pair * tiles, LANES), BF16),
        scratch_shapes=[
            pltpu.VMEM((channels * rows, LANES), F32),
            pltpu.VMEM((tiles, channels * rows, LANES), F32),
            pltpu.SemaphoreType.DMA((tiles,)),
        ],
        compiler_params=params(16),
        cost_estimate=cost(10**7, 4 * 10**6),
    )(product, h, factor_slab)
    grad = exchange(sent_grad)

    gate_normed, early_share = pl.pallas_call(
        gate_side_kernel,
        name="gate_side",
        grid=(tiles,),
        in_specs=[
            vmem, column_spec, column_spec, column_spec, row_spec, row_spec,
            whole((channels, channels)),
            pl.BlockSpec((channels, channels), lambda t: (0, 4)),
        ],
        out_specs=[column_spec, whole((slabs, 8, LANES))],
        out_shape=[
            pltpu.HBM((tiles, channels, cells), F32),
            pltpu.HBM((slabs, 8, LANES), BF16),
        ],
        scratch_shapes=[
            pltpu.VMEM((channels * rows, LANES), F32),
            pltpu.VMEM((channels, channels), F32),
            pltpu.VMEM((channels, channels), F32),
            pltpu.VMEM((slabs * 8, LANES), F32),
        ],
        compiler_params=params(24),
        cost_estimate=cost(6 * 10**8, 8 * 10**6),
    )(product, normed, mixed, gate_coef, out_gain, out_bias, out_weight, weight)
    gate_normed, early_share = pinned(gate_normed, early_share)

    height = 2 * pair * tiles
    sent_parts = pl.pallas_call(
        factor_grad_kernel,
        name="factor_grad",
        in_specs=[vmem, anywhere, anywhere],
        out_specs=vmem,
        out_shape=jax.ShapeDtypeStruct((slabs, height, LANES), BF16),
        scratch_shapes=[
            pltpu.VMEM((2, tokens, tokens), BF16),
            pltpu.VMEM((2, tokens, tokens), BF16),
            pltpu.VMEM((4, tokens, tokens), BF16),
            pltpu.SemaphoreType.DMA((4,)),
        ],
        compiler_params=params(20),
        cost_estimate=cost(11 * 10**8, 5 * 10**6),
    )(grad, factor_slab, early_share)
    parts = exchange(sent_parts)

    late_share = pl.pallas_call(
        proj_grad_kernel,
        name="proj_grad",
        grid=(tiles,),
        in_specs=[vmem, coef_spec, column_spec, whole((slabs, 8, LANES))],
        out_specs=whole((slabs, 16, LANES)),
        out_shape=pltpu.HBM((slabs, 16, LANES), BF16),
        scratch_shapes=[
            pltpu.VMEM((2, channels * rows, LANES), F32),
            pltpu.VMEM((4, channels, channels), F32),
            pltpu.VMEM((slabs * 8, LANES), F32),
        ],
        compiler_params=params(24),
        cost_estimate=cost(6 * 10**8, 8 * 10**6),
    )(parts, coef, normed, early_share)
    shares = exchange(late_share)

    pair_gradient = pl.pallas_call(
        pair_grad_kernel,
        name="pair_grad",
        grid=(tiles,),
        in_specs=[vmem, coef_spec, column_spec, cell_spec, row_spec, factor_weight_spec],
        out_specs=cell_spec,
        out_shape=pltpu.HBM((rows, tokens, channels), BF16),
        scratch_shapes=[pltpu.VMEM((2, channels * rows, LANES), F32)],
        compiler_params=params(24),
        cost_estimate=cost(6 * 10**8, 8 * 10**6),
    )(parts, coef, gate_normed, pair_hbm, gain, weight)

    held = channels // slabs
    input_gradient, output_gradient = pl.pallas_call(
        lambda *refs: weight_sum_kernel(*refs, tokens=tokens),
        name="weight_sum",
        in_specs=[vmem],
        out_specs=[whole((held, 5 * channels)), whole((held, channels))],
        out_shape=[
            pltpu.HBM((held, 5 * channels), F32),
            pltpu.HBM((held, channels), F32),
        ],
        compiler_params=params(16),
        cost_estimate=cost(10**5, 4 * 10**5),
    )(shares)
    return (pair_gradient, input_gradient, output_gradient)


def solution(mesh):
    return jax.shard_map(
        on_device,
        mesh=mesh,
        in_specs=(
            P(("cplx", "row"), None, None),
            P(("cplx", "row"), None, None),
            P("cplx"),
            P(),
            P(),
            P(),
            P(),
            P(),
            P(),
        ),
        out_specs=(
            P(("cplx", "row"), None, None),
            P(("cplx", "row"), None),
            P(("cplx", "row"), None),
        ),
        check_vma=False,
    )
```

```python
import jax
import jax.numpy as jnp
from jax import lax
from jax.experimental import pallas as pl
from jax.experimental.pallas import tpu as pltpu
from jax.sharding import PartitionSpec as P

epsilon = 1e-05
LANES = 128
F32 = jnp.float32
BF16 = jnp.bfloat16


def dot_nn(a, b):
    return lax.dot_general(a, b, (((1,), (0,)), ((), ())), preferred_element_type=F32)


def dot_nt(a, b):
    return lax.dot_general(a, b, (((1,), (1,)), ((), ())), preferred_element_type=F32)


def dot_tn(a, b):
    return lax.dot_general(a, b, (((0,), (0,)), ((), ())), preferred_element_type=F32)


def eye(size, dtype):
    rows = lax.broadcasted_iota(jnp.int32, (size, size), 0)
    cols = lax.broadcasted_iota(jnp.int32, (size, size), 1)
    return jnp.where(rows == cols, 1.0, 0.0).astype(F32).astype(dtype)


def as_column(row):
    return jnp.sum(eye(row.shape[1], F32) * row, axis=1, keepdims=True)


def turned(block):
    rows, lanes, channels = block.shape
    return dot_nt(eye(channels, BF16), block.reshape(rows * lanes, channels))


def norm_columns(values):
    average = jnp.mean(values, axis=0, keepdims=True)
    centered = values - average
    variance = jnp.mean(centered * centered, axis=0, keepdims=True)
    inverse = lax.rsqrt(variance + epsilon)
    return centered * inverse, inverse


def norm_columns_backward(upstream, scaled, inverse):
    first = jnp.mean(upstream, axis=0, keepdims=True)
    second = jnp.mean(upstream * scaled, axis=0, keepdims=True)
    return inverse * (upstream - first - scaled * second)


def normed_columns(block, gain_row, bias_row):
    scaled, inverse = norm_columns(turned(block))
    normed = (scaled * as_column(gain_row) + as_column(bias_row)).astype(BF16)
    return normed, scaled, inverse


def mask_row(start_ref, mask_ref, lane_mask, rows):
    lane_float = lane_mask.astype(F32)
    parts = [
        lane_float * mask_ref[start_ref[0] + row].astype(F32) for row in range(rows)
    ]
    return jnp.concatenate(parts, axis=1)


def front_kernel(
    start_ref, mask_ref, lane_mask_ref, x_ref, gain_ref, bias_ref, weight_ref, out_ref,
    turned_weight, spread,
):
    rows = x_ref.shape[0]
    channels = x_ref.shape[2]

    @pl.when(pl.program_id(0) == 0)
    def _():
        turned_weight[...] = weight_ref[...].astype(F32).T.astype(BF16)

    gain, bias = as_column(gain_ref[...]), as_column(bias_ref[...])
    lane_mask = lane_mask_ref[...].astype(F32)
    scaled, _ = norm_columns(turned(x_ref[...]))
    normed = (scaled * gain + bias).astype(BF16)
    masks = [lane_mask * mask_ref[start_ref[0] + row].astype(F32) for row in range(rows)]
    pair_mask = jnp.concatenate(masks, axis=1)
    for side in range(2):
        base = 2 * side * channels
        pre = dot_nn(turned_weight[base : base + 2 * channels, :], normed)
        factor = pair_mask * jax.nn.sigmoid(pre[channels:]) * pre[:channels]
        for row in range(rows):
            spread[side, pl.ds(row, channels, stride=rows), :] = factor[
                :, row * LANES : (row + 1) * LANES
            ]
    group = channels * rows // out_ref.shape[0]
    base = pl.multiple_of(pl.program_id(0) * 2 * group, 2 * group)
    for side in range(2):
        out_ref[:, pl.ds(base + side * group, group), :] = (
            spread[side].reshape(out_ref.shape[0], group, LANES).astype(BF16)
        )


def side_kernel(
    start_ref, mask_ref, lane_mask_ref, x_ref, cot_ref, gain_ref, bias_ref, weight_ref,
    out_gain_ref, out_weight_ref,
    h_ref, coef_ref, normed_ref, mixed_ref, gate_coef_ref,
    turned_weight,
):
    rows = x_ref.shape[0]
    channels = x_ref.shape[2]

    @pl.when(pl.program_id(0) == 0)
    def _():
        turned_weight[...] = weight_ref[...].astype(F32).T.astype(BF16)

    normed, _, _ = normed_columns(x_ref[...], gain_ref[...], bias_ref[...])
    normed_ref[0] = normed
    pair_mask = mask_row(start_ref, mask_ref, lane_mask_ref[...], rows)
    for side in range(2):
        base = 2 * side * channels
        pre = dot_nn(turned_weight[base : base + 2 * channels, :], normed)
        gate = jax.nn.sigmoid(pre[channels:])
        coef_ref[0, 2 * side] = (pair_mask * gate).astype(BF16)
        slope = pair_mask * pre[:channels] * gate * (1.0 - gate)
        coef_ref[0, 2 * side + 1] = slope.astype(BF16)
    out_gate = jax.nn.sigmoid(dot_nn(turned_weight[4 * channels :, :], normed))
    upstream = turned(cot_ref[...])
    mixed = (upstream * out_gate).astype(BF16)
    mixed_ref[0] = mixed
    gate_coef_ref[0] = upstream * out_gate * (1.0 - out_gate)
    h = dot_nn(out_weight_ref[...], mixed) * as_column(out_gain_ref[...])
    h = h - jnp.mean(h, axis=0, keepdims=True)
    for row in range(rows):
        h_ref[0, pl.ds(row, channels, stride=rows), :] = h[:, row * LANES : (row + 1) * LANES]


def unpack(recv_ref, base, rows):
    block = recv_ref[:, base : base + 2 * rows, :].astype(F32)
    slabs = block.shape[0]
    return [
        block[:, part * rows : (part + 1) * rows, :].reshape(slabs * rows, LANES).astype(BF16)
        for part in range(2)
    ]


def pack(first, second, slabs):
    rows = first.shape[0] // slabs
    parts = [part.reshape(slabs, rows, LANES) for part in (first, second)]
    return jnp.concatenate(parts, axis=1).astype(BF16)


def slab_unpack_kernel(recv_ref, out_ref):
    slabs = recv_ref.shape[0]
    tokens = out_ref.shape[1]
    rows = tokens // slabs
    for tile in range(tokens // LANES):
        for side in range(2):
            parts = unpack(recv_ref, (tile * 2 + side) * 2 * rows, rows)
            for part in range(2):
                out_ref[side * 2 + part, :, tile * LANES : (tile + 1) * LANES] = parts[part]


def product_kernel(recv_ref, out_ref, slab):
    slabs = recv_ref.shape[0]
    tokens = slab.shape[1]
    slab_unpack_kernel(recv_ref, slab)
    rows = tokens // slabs
    products = [dot_nt(slab[part], slab[2 + part]) for part in range(2)]
    for tile in range(tokens // LANES):
        cols = slice(tile * LANES, (tile + 1) * LANES)
        out_ref[:, tile * 2 * rows : (tile + 1) * 2 * rows, :] = pack(
            products[0][:, cols], products[1][:, cols], slabs
        )


def product_grad_kernel(recv_ref, h_hbm, factor_hbm, out_ref, held, h_ref, arrived):
    del factor_hbm
    step = pl.program_id(0)

    @pl.when(step == 0)
    def _():
        for tile in range(h_hbm.shape[0]):
            pltpu.make_async_copy(h_hbm.at[tile], h_ref.at[tile], arrived.at[tile]).start()

    slabs, group, _ = out_ref.shape
    rows = group // 2
    channels = 2 * slabs
    base = pl.multiple_of(step * group, group)
    chunk = 8
    size = 2 * chunk * rows

    def h_at(at):
        return h_ref[step, at * group : at * group + size, :].reshape(2 * chunk, rows, LANES)

    def held_at(at):
        return held[at * group : at * group + size, :].reshape(2 * chunk, rows, LANES)

    total = jnp.zeros((rows, LANES), F32)
    for at in range(0, slabs, chunk):
        block = recv_ref[at : at + chunk, pl.ds(base, group), :].astype(F32)
        held[at * group : at * group + size, :] = block.reshape(size, LANES)
        total = total + jnp.sum(block.reshape(2 * chunk, rows, LANES), axis=0)
    average = (total / channels)[None]
    pltpu.make_async_copy(h_hbm.at[step], h_ref.at[step], arrived.at[step]).wait()
    squares = jnp.zeros((rows, LANES), F32)
    cross = jnp.zeros((rows, LANES), F32)
    for at in range(0, slabs, chunk):
        centered = held_at(at) - average
        squares = squares + jnp.sum(centered * centered, axis=0)
        cross = cross + jnp.sum(centered * h_at(at), axis=0)
    inverse = lax.rsqrt(squares / channels + epsilon)
    slope = inverse * inverse * inverse * (cross / channels)
    inverse, slope = inverse[None], slope[None]
    for at in range(0, slabs, chunk):
        grad = inverse * h_at(at) - (held_at(at) - average) * slope
        out_ref[at : at + chunk] = grad.reshape(chunk, group, LANES).astype(BF16)


def gather_rows(spread, channels, rows):
    return jnp.concatenate(
        [spread[pl.ds(row, channels, stride=rows), :] for row in range(rows)], axis=1
    )


def gate_side_kernel(
    recv_ref, normed_ref, mixed_ref, gate_coef_ref, out_gain_ref, out_bias_ref,
    out_weight_ref, gate_weight_ref,
    gate_normed_ref, share_ref,
    spread, gate_term, out_term, laid,
):
    step = pl.program_id(0)
    channels = normed_ref.shape[1]
    rows = normed_ref.shape[2] // LANES
    group = channels * rows // recv_ref.shape[0]
    block = recv_ref[:, pl.ds(pl.multiple_of(step * group, group), group), :]

    @pl.when(step == 0)
    def _():
        gate_term[...] = jnp.zeros_like(gate_term)
        out_term[...] = jnp.zeros_like(out_term)

    spread[...] = block.astype(F32).reshape(channels * rows, LANES)
    product = gather_rows(spread, channels, rows)
    scaled, _ = norm_columns(product)
    normed_out = (scaled * as_column(out_gain_ref[...]) + as_column(out_bias_ref[...])).astype(BF16)
    projected = dot_tn(out_weight_ref[...], normed_out)
    gate_grad = (projected * gate_coef_ref[0]).astype(BF16)
    gate_normed_ref[0] = dot_nn(gate_weight_ref[...], gate_grad)
    gate_term[...] += dot_nt(normed_ref[0], gate_grad)
    out_term[...] += dot_nt(normed_out, mixed_ref[0])

    @pl.when(step == pl.num_programs(0) - 1)
    def _():
        half = channels // 2
        for which, term in enumerate((gate_term, out_term)):
            for part in range(2):
                value = term[pl.ds(part, half, stride=2), :]
                high = value.astype(BF16).astype(F32)
                laid[pl.ds(part * 4 + which * 2, half, stride=8), :] = high
                laid[pl.ds(part * 4 + which * 2 + 1, half, stride=8), :] = value - high
        share_ref[...] = laid[...].reshape(half, 8, LANES).astype(BF16)


def factor_grad_kernel(
    recv_ref, factor_hbm, early_hbm, out_ref, slab, turned_slab, factor, arrived
):
    del early_hbm
    slabs = recv_ref.shape[0]
    tokens = slab.shape[1]
    rows = tokens // slabs
    loads = [
        pltpu.make_async_copy(factor_hbm.at[which], factor.at[which], arrived.at[which])
        for which in range(4)
    ]
    for which in (2, 3, 0, 1):
        loads[which].start()
    for tile in range(tokens // LANES):
        parts = unpack(recv_ref, tile * 2 * rows, rows)
        for part in range(2):
            slab[part, :, tile * LANES : (tile + 1) * LANES] = parts[part]
    for side in range(2):
        for part in range(2):
            loads[2 * (1 - side) + part].wait()
        if side == 0:
            for part in range(2):
                turned_slab[part] = slab[part].T
        source = slab if side == 0 else turned_slab
        grads = [dot_nn(source[part], factor[2 * (1 - side) + part]) for part in range(2)]
        for tile in range(tokens // LANES):
            cols = slice(tile * LANES, (tile + 1) * LANES)
            base = (tile * 2 + side) * 2 * rows
            out_ref[:, base : base + 2 * rows, :] = pack(
                grads[0][:, cols], grads[1][:, cols], slabs
            )


def spread_parts(recv_ref, spread, rows):
    step = pl.program_id(0)
    channels = spread.shape[1] // rows
    group = channels * rows // recv_ref.shape[0]
    base = pl.multiple_of(step * 2 * group, 2 * group)
    for side in range(2):
        spread[side] = (
            recv_ref[:, pl.ds(base + side * group, group), :]
            .astype(F32)
            .reshape(channels * rows, LANES)
        )


def proj_blocks(recv_ref, coef_ref, spread, rows):
    channels = coef_ref.shape[2]
    spread_parts(recv_ref, spread, rows)
    blocks = []
    for side in range(2):
        grad = gather_rows(spread.at[side], channels, rows).astype(BF16)
        for part in range(2):
            blocks.append(grad * coef_ref[0, 2 * side + part])
    return blocks


def proj_grad_kernel(
    recv_ref, coef_ref, normed_ref, early_ref, share_ref, spread, term, laid
):
    step = pl.program_id(0)
    channels = normed_ref.shape[1]
    rows = normed_ref.shape[2] // LANES

    @pl.when(step == 0)
    def _():
        term[...] = jnp.zeros_like(term)

    spread_parts(recv_ref, spread, rows)
    for side in range(2):
        both = None
        for row in range(0, rows, 4):
            cols = slice(row * LANES, (row + 4) * LANES)
            grad = jnp.concatenate(
                [spread[side, pl.ds(at, channels, stride=rows), :] for at in range(row, row + 4)],
                axis=1,
            )
            grad = grad.astype(BF16)
            values = [grad * coef_ref[step, 2 * side + part, :, cols] for part in range(2)]
            piece = dot_nt(normed_ref[step, :, cols], jnp.concatenate(values, axis=0))
            both = piece if both is None else both + piece
        for part in range(2):
            term[2 * side + part] += both[:, part * channels : (part + 1) * channels]

    @pl.when(step == pl.num_programs(0) - 1)
    def _():
        half = channels // 2
        for part in range(2):
            for block in range(4):
                laid[pl.ds(part * 4 + block, half, stride=8), :] = term[
                    block, pl.ds(part, half, stride=2), :
                ]
        late = laid[...].reshape(half, 8, LANES)
        early = early_ref[...].astype(F32)
        share_ref[...] = jnp.concatenate([late, early], axis=1).astype(BF16)


def pair_grad_kernel(
    recv_ref, coef_ref, gate_normed_ref, x_ref, gain_ref, weight_ref, out_ref, spread
):
    rows = x_ref.shape[0]
    blocks = proj_blocks(recv_ref, coef_ref, spread, rows)
    scaled, inverse = norm_columns(turned(x_ref[...]))
    normed_grad = dot_nn(weight_ref[...], jnp.concatenate(blocks, axis=0)) + gate_normed_ref[0]
    grad = norm_columns_backward(normed_grad * as_column(gain_ref[...]), scaled, inverse)
    for row in range(rows):
        out_ref[row] = grad[:, row * LANES : (row + 1) * LANES].T.astype(BF16)


def weight_sum_kernel(recv_ref, in_ref, out_ref, *, tokens):
    total = jnp.sum(recv_ref[...].astype(F32), axis=0) / tokens
    for part in range(2):
        for block in range(4):
            at = part * 4 + block
            in_ref[part : part + 1, block * LANES : (block + 1) * LANES] = total[at : at + 1]
        at = 8 + part * 4
        in_ref[part : part + 1, 4 * LANES :] = total[at : at + 1] + total[at + 1 : at + 2]
        out_ref[part : part + 1, :] = total[at + 2 : at + 3] + total[at + 3 : at + 4]


def whole(shape):
    return pl.BlockSpec(shape, lambda *_: (0,) * len(shape))


def exchange(values):
    return lax.all_to_all(values, "row", split_axis=0, concat_axis=0, tiled=True)


def params(megabytes):
    return pltpu.CompilerParams(vmem_limit_bytes=megabytes * 1024 * 1024)


def pinned(*arrays):
    return [pltpu.with_memory_space_constraint(array, pltpu.HBM) for array in arrays]


def cost(flops, moved):
    return pl.CostEstimate(flops=flops, bytes_accessed=moved, transcendentals=0)


def on_device(
    pair_state,
    cotangent,
    token_mask,
    input_gain,
    input_bias,
    input_weight,
    output_gain,
    output_bias,
    output_weight,
):
    rows, tokens, channels = pair_state.shape
    slabs = lax.axis_size("row")
    tiles = tokens // LANES
    cells = rows * LANES
    start = (lax.axis_index("row") * rows).astype(jnp.int32).reshape(1)
    lane_mask = token_mask.reshape(1, tokens)
    gain, bias = input_gain.reshape(1, channels), input_bias.reshape(1, channels)
    out_gain, out_bias = output_gain.reshape(1, channels), output_bias.reshape(1, channels)
    smem = pl.BlockSpec(memory_space=pltpu.SMEM)
    lane_spec = pl.BlockSpec((1, LANES), lambda t: (0, t))
    cell_spec = pl.BlockSpec((rows, LANES, channels), lambda t: (0, t, 0))
    row_spec = whole((1, channels))
    column_spec = pl.BlockSpec((1, channels, cells), lambda t: (t, 0, 0))

    def wire_spec(height):
        return pl.BlockSpec((slabs, height, LANES), lambda t: (0, t, 0))

    pair = 2 * rows
    vmem = pl.BlockSpec(memory_space=pltpu.VMEM)
    anywhere = pl.BlockSpec(memory_space=pl.ANY)
    h_spec = pl.BlockSpec((1, channels * rows, LANES), lambda t: (t, 0, 0))
    coef_spec = pl.BlockSpec((1, 4, channels, cells), lambda t: (t, 0, 0, 0))
    factor_weight_spec = pl.BlockSpec((channels, 4 * channels), lambda t: (0, 0))
    pair_hbm, cot_hbm, lane_hbm, gain, bias, out_gain, out_bias, weight, out_weight = pinned(
        pair_state, cotangent, lane_mask, gain, bias, out_gain, out_bias, input_weight, output_weight
    )

    sent_factors = pl.pallas_call(
        front_kernel,
        name="front",
        grid=(tiles,),
        in_specs=[
            smem, smem, lane_spec, cell_spec, row_spec, row_spec, factor_weight_spec,
        ],
        out_specs=vmem,
        out_shape=jax.ShapeDtypeStruct((slabs, 2 * pair * tiles, LANES), BF16),
        scratch_shapes=[
            pltpu.VMEM((4 * channels, channels), BF16),
            pltpu.VMEM((2, channels * rows, LANES), F32),
        ],
        compiler_params=params(16),
        cost_estimate=cost(6 * 10**8, 4 * 10**6),
    )(start, token_mask, lane_hbm, pair_hbm, gain, bias, weight)
    factors = exchange(sent_factors)

    h, coef, normed, mixed, gate_coef = pl.pallas_call(
        side_kernel,
        name="side",
        grid=(tiles,),
        in_specs=[
            smem, smem, lane_spec, cell_spec, cell_spec, row_spec, row_spec,
            whole((channels, 5 * channels)), row_spec, whole((channels, channels)),
        ],
        out_specs=[h_spec, coef_spec, column_spec, column_spec, column_spec],
        out_shape=[
            pltpu.HBM((tiles, channels * rows, LANES), F32),
            pltpu.HBM((tiles, 4, channels, cells), BF16),
            pltpu.HBM((tiles, channels, cells), BF16),
            pltpu.HBM((tiles, channels, cells), BF16),
            pltpu.HBM((tiles, channels, cells), F32),
        ],
        scratch_shapes=[pltpu.VMEM((5 * channels, channels), BF16)],
        compiler_params=params(40),
        cost_estimate=cost(12 * 10**8, 16 * 10**6),
    )(start, token_mask, lane_hbm, pair_hbm, cot_hbm, gain, bias, weight, out_gain, out_weight)
    near = (coef, normed)
    h, coef, normed, mixed, gate_coef = pinned(h, coef, normed, mixed, gate_coef)

    sent_product = pl.pallas_call(
        product_kernel,
        name="product",
        in_specs=[vmem],
        out_specs=whole((slabs, pair * tiles, LANES)),
        out_shape=pltpu.HBM((slabs, pair * tiles, LANES), BF16),
        scratch_shapes=[pltpu.VMEM((4, tokens, tokens), BF16)],
        compiler_params=params(20),
        cost_estimate=cost(6 * 10**8, 3 * 10**6),
    )(factors)
    product = exchange(sent_product)

    factor_slab = pl.pallas_call(
        slab_unpack_kernel,
        name="slabs",
        in_specs=[vmem],
        out_specs=whole((4, tokens, tokens)),
        out_shape=pltpu.HBM((4, tokens, tokens), BF16),
        compiler_params=params(20),
        cost_estimate=cost(10**6, 4 * 10**6),
    )(factors)
    (factor_slab,) = pinned(factor_slab)

    sent_grad = pl.pallas_call(
        product_grad_kernel,
        name="product_grad",
        grid=(tiles,),
        in_specs=[vmem, anywhere, anywhere],
        out_specs=wire_spec(pair),
        out_shape=pltpu.HBM((slabs, pair * tiles, LANES), BF16),
        scratch_shapes=[
            pltpu.VMEM((channels * rows, LANES), F32),
            pltpu.VMEM((tiles, channels * rows, LANES), F32),
            pltpu.SemaphoreType.DMA((tiles,)),
        ],
        compiler_params=params(16),
        cost_estimate=cost(10**7, 4 * 10**6),
    )(product, h, factor_slab)
    grad = exchange(sent_grad)

    gate_normed, early_share = pl.pallas_call(
        gate_side_kernel,
        name="gate_side",
        grid=(tiles,),
        in_specs=[
            vmem, column_spec, column_spec, column_spec, row_spec, row_spec,
            whole((channels, channels)),
            pl.BlockSpec((channels, channels), lambda t: (0, 4)),
        ],
        out_specs=[column_spec, whole((slabs, 8, LANES))],
        out_shape=[
            pltpu.HBM((tiles, channels, cells), F32),
            pltpu.HBM((slabs, 8, LANES), BF16),
        ],
        scratch_shapes=[
            pltpu.VMEM((channels * rows, LANES), F32),
            pltpu.VMEM((channels, channels), F32),
            pltpu.VMEM((channels, channels), F32),
            pltpu.VMEM((slabs * 8, LANES), F32),
        ],
        compiler_params=params(24),
        cost_estimate=cost(6 * 10**8, 8 * 10**6),
    )(product, normed, mixed, gate_coef, out_gain, out_bias, out_weight, weight)
    gate_normed, early_share = pinned(gate_normed, early_share)

    height = 2 * pair * tiles
    sent_parts = pl.pallas_call(
        factor_grad_kernel,
        name="factor_grad",
        in_specs=[vmem, anywhere, anywhere],
        out_specs=vmem,
        out_shape=jax.ShapeDtypeStruct((slabs, height, LANES), BF16),
        scratch_shapes=[
            pltpu.VMEM((2, tokens, tokens), BF16),
            pltpu.VMEM((2, tokens, tokens), BF16),
            pltpu.VMEM((4, tokens, tokens), BF16),
            pltpu.SemaphoreType.DMA((4,)),
        ],
        compiler_params=params(20),
        cost_estimate=cost(11 * 10**8, 5 * 10**6),
    )(grad, factor_slab, early_share)
    parts = exchange(sent_parts)

    late_share = pl.pallas_call(
        proj_grad_kernel,
        name="proj_grad",
        grid=(tiles,),
        in_specs=[vmem, vmem, vmem, whole((slabs, 8, LANES))],
        out_specs=whole((slabs, 16, LANES)),
        out_shape=pltpu.HBM((slabs, 16, LANES), BF16),
        scratch_shapes=[
            pltpu.VMEM((2, channels * rows, LANES), F32),
            pltpu.VMEM((4, channels, channels), F32),
            pltpu.VMEM((slabs * 8, LANES), F32),
        ],
        compiler_params=params(24),
        cost_estimate=cost(6 * 10**8, 8 * 10**6),
    )(parts, *near, early_share)
    shares = exchange(late_share)

    pair_gradient = pl.pallas_call(
        pair_grad_kernel,
        name="pair_grad",
        grid=(tiles,),
        in_specs=[vmem, coef_spec, column_spec, cell_spec, row_spec, factor_weight_spec],
        out_specs=cell_spec,
        out_shape=pltpu.HBM((rows, tokens, channels), BF16),
        scratch_shapes=[pltpu.VMEM((2, channels * rows, LANES), F32)],
        compiler_params=params(24),
        cost_estimate=cost(6 * 10**8, 8 * 10**6),
    )(parts, coef, gate_normed, pair_hbm, gain, weight)

    held = channels // slabs
    input_gradient, output_gradient = pl.pallas_call(
        lambda *refs: weight_sum_kernel(*refs, tokens=tokens),
        name="weight_sum",
        in_specs=[vmem],
        out_specs=[whole((held, 5 * channels)), whole((held, channels))],
        out_shape=[
            pltpu.HBM((held, 5 * channels), F32),
            pltpu.HBM((held, channels), F32),
        ],
        compiler_params=params(16),
        cost_estimate=cost(10**5, 4 * 10**5),
    )(shares)
    return (pair_gradient, input_gradient, output_gradient)


def solution(mesh):
    return jax.shard_map(
        on_device,
        mesh=mesh,
        in_specs=(
            P(("cplx", "row"), None, None),
            P(("cplx", "row"), None, None),
            P("cplx"),
            P(),
            P(),
            P(),
            P(),
            P(),
            P(),
        ),
        out_specs=(
            P(("cplx", "row"), None, None),
            P(("cplx", "row"), None),
            P(("cplx", "row"), None),
        ),
        check_vma=False,
    )
```

```python
import jax
import jax.numpy as jnp
from jax import lax
from jax.experimental import pallas as pl
from jax.experimental.pallas import tpu as pltpu
from jax.sharding import PartitionSpec as P

epsilon = 1e-05
LANES = 128
F32 = jnp.float32
BF16 = jnp.bfloat16


def dot_nn(a, b):
    return lax.dot_general(a, b, (((1,), (0,)), ((), ())), preferred_element_type=F32)


def dot_nt(a, b):
    return lax.dot_general(a, b, (((1,), (1,)), ((), ())), preferred_element_type=F32)


def dot_tn(a, b):
    return lax.dot_general(a, b, (((0,), (0,)), ((), ())), preferred_element_type=F32)


def eye(size, dtype):
    rows = lax.broadcasted_iota(jnp.int32, (size, size), 0)
    cols = lax.broadcasted_iota(jnp.int32, (size, size), 1)
    return jnp.where(rows == cols, 1.0, 0.0).astype(F32).astype(dtype)


def as_column(row):
    return jnp.sum(eye(row.shape[1], F32) * row, axis=1, keepdims=True)


def turned(block):
    rows, lanes, channels = block.shape
    return dot_nt(eye(channels, BF16), block.reshape(rows * lanes, channels))


def norm_columns(values):
    average = jnp.mean(values, axis=0, keepdims=True)
    centered = values - average
    variance = jnp.mean(centered * centered, axis=0, keepdims=True)
    inverse = lax.rsqrt(variance + epsilon)
    return centered * inverse, inverse


def norm_columns_backward(upstream, scaled, inverse):
    first = jnp.mean(upstream, axis=0, keepdims=True)
    second = jnp.mean(upstream * scaled, axis=0, keepdims=True)
    return inverse * (upstream - first - scaled * second)


def normed_columns(block, gain_row, bias_row):
    scaled, inverse = norm_columns(turned(block))
    normed = (scaled * as_column(gain_row) + as_column(bias_row)).astype(BF16)
    return normed, scaled, inverse


def mask_row(start_ref, mask_ref, lane_mask, rows):
    lane_float = lane_mask.astype(F32)
    parts = [
        lane_float * mask_ref[start_ref[0] + row].astype(F32) for row in range(rows)
    ]
    return jnp.concatenate(parts, axis=1)


def front_kernel(
    start_ref, mask_ref, lane_mask_ref, x_ref, gain_ref, bias_ref, weight_ref, out_ref,
    turned_weight, spread,
):
    rows = x_ref.shape[0]
    channels = x_ref.shape[2]

    @pl.when(pl.program_id(0) == 0)
    def _():
        turned_weight[...] = weight_ref[...].astype(F32).T.astype(BF16)

    gain, bias = as_column(gain_ref[...]), as_column(bias_ref[...])
    lane_mask = lane_mask_ref[...].astype(F32)
    scaled, _ = norm_columns(turned(x_ref[...]))
    normed = (scaled * gain + bias).astype(BF16)
    masks = [lane_mask * mask_ref[start_ref[0] + row].astype(F32) for row in range(rows)]
    pair_mask = jnp.concatenate(masks, axis=1)
    for side in range(2):
        base = 2 * side * channels
        pre = dot_nn(turned_weight[base : base + 2 * channels, :], normed)
        factor = pair_mask * jax.nn.sigmoid(pre[channels:]) * pre[:channels]
        for row in range(rows):
            spread[side, pl.ds(row, channels, stride=rows), :] = factor[
                :, row * LANES : (row + 1) * LANES
            ]
    group = channels * rows // out_ref.shape[0]
    base = pl.multiple_of(pl.program_id(0) * 2 * group, 2 * group)
    for side in range(2):
        out_ref[:, pl.ds(base + side * group, group), :] = (
            spread[side].reshape(out_ref.shape[0], group, LANES).astype(BF16)
        )


def side_kernel(
    start_ref, mask_ref, lane_mask_ref, x_ref, cot_ref, gain_ref, bias_ref, weight_ref,
    out_gain_ref, out_weight_ref,
    h_ref, coef_ref, normed_ref, mixed_ref, gate_coef_ref,
    turned_weight,
):
    rows = x_ref.shape[0]
    channels = x_ref.shape[2]

    @pl.when(pl.program_id(0) == 0)
    def _():
        turned_weight[...] = weight_ref[...].astype(F32).T.astype(BF16)

    normed, _, _ = normed_columns(x_ref[...], gain_ref[...], bias_ref[...])
    normed_ref[0] = normed
    pair_mask = mask_row(start_ref, mask_ref, lane_mask_ref[...], rows)
    for side in range(2):
        base = 2 * side * channels
        pre = dot_nn(turned_weight[base : base + 2 * channels, :], normed)
        gate = jax.nn.sigmoid(pre[channels:])
        coef_ref[0, 2 * side] = (pair_mask * gate).astype(BF16)
        slope = pair_mask * pre[:channels] * gate * (1.0 - gate)
        coef_ref[0, 2 * side + 1] = slope.astype(BF16)
    out_gate = jax.nn.sigmoid(dot_nn(turned_weight[4 * channels :, :], normed))
    upstream = turned(cot_ref[...])
    mixed = (upstream * out_gate).astype(BF16)
    mixed_ref[0] = mixed
    gate_coef_ref[0] = upstream * out_gate * (1.0 - out_gate)
    h = dot_nn(out_weight_ref[...], mixed) * as_column(out_gain_ref[...])
    h = h - jnp.mean(h, axis=0, keepdims=True)
    for row in range(rows):
        h_ref[0, pl.ds(row, channels, stride=rows), :] = h[:, row * LANES : (row + 1) * LANES]


def unpack(recv_ref, base, rows):
    block = recv_ref[:, base : base + 2 * rows, :].astype(F32)
    slabs = block.shape[0]
    return [
        block[:, part * rows : (part + 1) * rows, :].reshape(slabs * rows, LANES).astype(BF16)
        for part in range(2)
    ]


def pack(first, second, slabs):
    rows = first.shape[0] // slabs
    parts = [part.reshape(slabs, rows, LANES) for part in (first, second)]
    return jnp.concatenate(parts, axis=1).astype(BF16)


def slab_unpack_kernel(recv_ref, out_ref):
    slabs = recv_ref.shape[0]
    tokens = out_ref.shape[1]
    rows = tokens // slabs
    for tile in range(tokens // LANES):
        for side in range(2):
            parts = unpack(recv_ref, (tile * 2 + side) * 2 * rows, rows)
            for part in range(2):
                out_ref[side * 2 + part, :, tile * LANES : (tile + 1) * LANES] = parts[part]


def product_kernel(recv_ref, out_hbm, slab, out_ref, sent):
    slabs = recv_ref.shape[0]
    tokens = slab.shape[1]
    slab_unpack_kernel(recv_ref, slab)
    rows = tokens // slabs
    products = [dot_nt(slab[part], slab[2 + part]) for part in range(2)]
    tiles = tokens // LANES
    group = 2 * rows
    stores = []
    for tile in range(tiles):
        cols = slice(tile * LANES, (tile + 1) * LANES)
        out_ref[tile] = pack(products[0][:, cols], products[1][:, cols], slabs)
        stores.append(
            pltpu.make_async_copy(
                out_ref.at[tile], out_hbm.at[:, pl.ds(tile * group, group), :], sent.at[tile]
            )
        )
        stores[tile].start()
    for store in stores:
        store.wait()


def product_grad_kernel(recv_ref, h_hbm, factor_hbm, out_ref, held, h_ref, arrived):
    del factor_hbm
    step = pl.program_id(0)

    @pl.when(step == 0)
    def _():
        for tile in range(h_hbm.shape[0]):
            pltpu.make_async_copy(h_hbm.at[tile], h_ref.at[tile], arrived.at[tile]).start()

    slabs, group, _ = out_ref.shape
    rows = group // 2
    channels = 2 * slabs
    base = pl.multiple_of(step * group, group)
    chunk = 8
    size = 2 * chunk * rows

    def h_at(at):
        return h_ref[step, at * group : at * group + size, :].reshape(2 * chunk, rows, LANES)

    def held_at(at):
        return held[at * group : at * group + size, :].reshape(2 * chunk, rows, LANES)

    total = jnp.zeros((rows, LANES), F32)
    for at in range(0, slabs, chunk):
        block = recv_ref[at : at + chunk, pl.ds(base, group), :].astype(F32)
        held[at * group : at * group + size, :] = block.reshape(size, LANES)
        total = total + jnp.sum(block.reshape(2 * chunk, rows, LANES), axis=0)
    average = (total / channels)[None]
    pltpu.make_async_copy(h_hbm.at[step], h_ref.at[step], arrived.at[step]).wait()
    squares = jnp.zeros((rows, LANES), F32)
    cross = jnp.zeros((rows, LANES), F32)
    for at in range(0, slabs, chunk):
        centered = held_at(at) - average
        squares = squares + jnp.sum(centered * centered, axis=0)
        cross = cross + jnp.sum(centered * h_at(at), axis=0)
    inverse = lax.rsqrt(squares / channels + epsilon)
    slope = inverse * inverse * inverse * (cross / channels)
    inverse, slope = inverse[None], slope[None]
    for at in range(0, slabs, chunk):
        grad = inverse * h_at(at) - (held_at(at) - average) * slope
        out_ref[at : at + chunk] = grad.reshape(chunk, group, LANES).astype(BF16)


def gather_rows(spread, channels, rows):
    return jnp.concatenate(
        [spread[pl.ds(row, channels, stride=rows), :] for row in range(rows)], axis=1
    )


def gate_side_kernel(
    recv_ref, normed_ref, mixed_ref, gate_coef_ref, out_gain_ref, out_bias_ref,
    out_weight_ref, gate_weight_ref,
    gate_normed_ref, share_ref,
    spread, gate_term, out_term, laid,
):
    step = pl.program_id(0)
    channels = normed_ref.shape[1]
    rows = normed_ref.shape[2] // LANES
    group = channels * rows // recv_ref.shape[0]
    block = recv_ref[:, pl.ds(pl.multiple_of(step * group, group), group), :]

    @pl.when(step == 0)
    def _():
        gate_term[...] = jnp.zeros_like(gate_term)
        out_term[...] = jnp.zeros_like(out_term)

    spread[...] = block.astype(F32).reshape(channels * rows, LANES)
    product = gather_rows(spread, channels, rows)
    scaled, _ = norm_columns(product)
    normed_out = (scaled * as_column(out_gain_ref[...]) + as_column(out_bias_ref[...])).astype(BF16)
    projected = dot_tn(out_weight_ref[...], normed_out)
    gate_grad = (projected * gate_coef_ref[0]).astype(BF16)
    gate_normed_ref[0] = dot_nn(gate_weight_ref[...], gate_grad)
    gate_term[...] += dot_nt(normed_ref[0], gate_grad)
    out_term[...] += dot_nt(normed_out, mixed_ref[0])

    @pl.when(step == pl.num_programs(0) - 1)
    def _():
        half = channels // 2
        for which, term in enumerate((gate_term, out_term)):
            for part in range(2):
                value = term[pl.ds(part, half, stride=2), :]
                high = value.astype(BF16).astype(F32)
                laid[pl.ds(part * 4 + which * 2, half, stride=8), :] = high
                laid[pl.ds(part * 4 + which * 2 + 1, half, stride=8), :] = value - high
        share_ref[...] = laid[...].reshape(half, 8, LANES).astype(BF16)


def factor_grad_kernel(
    recv_ref, factor_hbm, early_hbm, out_ref, slab, turned_slab, factor, arrived
):
    del early_hbm
    slabs = recv_ref.shape[0]
    tokens = slab.shape[1]
    rows = tokens // slabs
    loads = [
        pltpu.make_async_copy(factor_hbm.at[which], factor.at[which], arrived.at[which])
        for which in range(4)
    ]
    for which in (2, 3, 0, 1):
        loads[which].start()
    for tile in range(tokens // LANES):
        parts = unpack(recv_ref, tile * 2 * rows, rows)
        for part in range(2):
            slab[part, :, tile * LANES : (tile + 1) * LANES] = parts[part]
    for side in range(2):
        for part in range(2):
            loads[2 * (1 - side) + part].wait()
        if side == 0:
            for part in range(2):
                turned_slab[part] = slab[part].T
        source = slab if side == 0 else turned_slab
        grads = [dot_nn(source[part], factor[2 * (1 - side) + part]) for part in range(2)]
        for tile in range(tokens // LANES):
            cols = slice(tile * LANES, (tile + 1) * LANES)
            base = (tile * 2 + side) * 2 * rows
            out_ref[:, base : base + 2 * rows, :] = pack(
                grads[0][:, cols], grads[1][:, cols], slabs
            )


def spread_parts(recv_ref, spread, rows):
    step = pl.program_id(0)
    channels = spread.shape[1] // rows
    group = channels * rows // recv_ref.shape[0]
    base = pl.multiple_of(step * 2 * group, 2 * group)
    for side in range(2):
        spread[side] = (
            recv_ref[:, pl.ds(base + side * group, group), :]
            .astype(F32)
            .reshape(channels * rows, LANES)
        )


def proj_blocks(recv_ref, coef_ref, spread, rows):
    channels = coef_ref.shape[2]
    spread_parts(recv_ref, spread, rows)
    blocks = []
    for side in range(2):
        grad = gather_rows(spread.at[side], channels, rows).astype(BF16)
        for part in range(2):
            blocks.append(grad * coef_ref[0, 2 * side + part])
    return blocks


def proj_grad_kernel(
    recv_ref, coef_ref, normed_ref, early_ref, share_ref, spread, term, laid
):
    step = pl.program_id(0)
    channels = normed_ref.shape[1]
    rows = normed_ref.shape[2] // LANES

    @pl.when(step == 0)
    def _():
        term[...] = jnp.zeros_like(term)

    spread_parts(recv_ref, spread, rows)
    for side in range(2):
        both = None
        for row in range(0, rows, 4):
            cols = slice(row * LANES, (row + 4) * LANES)
            grad = jnp.concatenate(
                [spread[side, pl.ds(at, channels, stride=rows), :] for at in range(row, row + 4)],
                axis=1,
            )
            grad = grad.astype(BF16)
            values = [grad * coef_ref[step, 2 * side + part, :, cols] for part in range(2)]
            piece = dot_nt(normed_ref[step, :, cols], jnp.concatenate(values, axis=0))
            both = piece if both is None else both + piece
        for part in range(2):
            term[2 * side + part] += both[:, part * channels : (part + 1) * channels]

    @pl.when(step == pl.num_programs(0) - 1)
    def _():
        half = channels // 2
        for part in range(2):
            for block in range(4):
                laid[pl.ds(part * 4 + block, half, stride=8), :] = term[
                    block, pl.ds(part, half, stride=2), :
                ]
        late = laid[...].reshape(half, 8, LANES)
        early = early_ref[...].astype(F32)
        share_ref[...] = jnp.concatenate([late, early], axis=1).astype(BF16)


def pair_grad_kernel(
    recv_ref, coef_ref, gate_normed_ref, x_ref, gain_ref, weight_ref, out_ref, spread
):
    rows = x_ref.shape[0]
    blocks = proj_blocks(recv_ref, coef_ref, spread, rows)
    scaled, inverse = norm_columns(turned(x_ref[...]))
    normed_grad = dot_nn(weight_ref[...], jnp.concatenate(blocks, axis=0)) + gate_normed_ref[0]
    grad = norm_columns_backward(normed_grad * as_column(gain_ref[...]), scaled, inverse)
    for row in range(rows):
        out_ref[row] = grad[:, row * LANES : (row + 1) * LANES].T.astype(BF16)


def weight_sum_kernel(recv_ref, in_ref, out_ref, *, tokens):
    total = jnp.sum(recv_ref[...].astype(F32), axis=0) / tokens
    for part in range(2):
        for block in range(4):
            at = part * 4 + block
            in_ref[part : part + 1, block * LANES : (block + 1) * LANES] = total[at : at + 1]
        at = 8 + part * 4
        in_ref[part : part + 1, 4 * LANES :] = total[at : at + 1] + total[at + 1 : at + 2]
        out_ref[part : part + 1, :] = total[at + 2 : at + 3] + total[at + 3 : at + 4]


def whole(shape):
    return pl.BlockSpec(shape, lambda *_: (0,) * len(shape))


def exchange(values):
    return lax.all_to_all(values, "row", split_axis=0, concat_axis=0, tiled=True)


def params(megabytes):
    return pltpu.CompilerParams(vmem_limit_bytes=megabytes * 1024 * 1024)


def pinned(*arrays):
    return [pltpu.with_memory_space_constraint(array, pltpu.HBM) for array in arrays]


def cost(flops, moved):
    return pl.CostEstimate(flops=flops, bytes_accessed=moved, transcendentals=0)


def on_device(
    pair_state,
    cotangent,
    token_mask,
    input_gain,
    input_bias,
    input_weight,
    output_gain,
    output_bias,
    output_weight,
):
    rows, tokens, channels = pair_state.shape
    slabs = lax.axis_size("row")
    tiles = tokens // LANES
    cells = rows * LANES
    start = (lax.axis_index("row") * rows).astype(jnp.int32).reshape(1)
    lane_mask = token_mask.reshape(1, tokens)
    gain, bias = input_gain.reshape(1, channels), input_bias.reshape(1, channels)
    out_gain, out_bias = output_gain.reshape(1, channels), output_bias.reshape(1, channels)
    smem = pl.BlockSpec(memory_space=pltpu.SMEM)
    lane_spec = pl.BlockSpec((1, LANES), lambda t: (0, t))
    cell_spec = pl.BlockSpec((rows, LANES, channels), lambda t: (0, t, 0))
    row_spec = whole((1, channels))
    column_spec = pl.BlockSpec((1, channels, cells), lambda t: (t, 0, 0))

    def wire_spec(height):
        return pl.BlockSpec((slabs, height, LANES), lambda t: (0, t, 0))

    pair = 2 * rows
    vmem = pl.BlockSpec(memory_space=pltpu.VMEM)
    anywhere = pl.BlockSpec(memory_space=pl.ANY)
    h_spec = pl.BlockSpec((1, channels * rows, LANES), lambda t: (t, 0, 0))
    coef_spec = pl.BlockSpec((1, 4, channels, cells), lambda t: (t, 0, 0, 0))
    factor_weight_spec = pl.BlockSpec((channels, 4 * channels), lambda t: (0, 0))
    pair_hbm, cot_hbm, lane_hbm, gain, bias, out_gain, out_bias, weight, out_weight = pinned(
        pair_state, cotangent, lane_mask, gain, bias, out_gain, out_bias, input_weight, output_weight
    )

    sent_factors = pl.pallas_call(
        front_kernel,
        name="front",
        grid=(tiles,),
        in_specs=[
            smem, smem, lane_spec, cell_spec, row_spec, row_spec, factor_weight_spec,
        ],
        out_specs=vmem,
        out_shape=jax.ShapeDtypeStruct((slabs, 2 * pair * tiles, LANES), BF16),
        scratch_shapes=[
            pltpu.VMEM((4 * channels, channels), BF16),
            pltpu.VMEM((2, channels * rows, LANES), F32),
        ],
        compiler_params=params(16),
        cost_estimate=cost(6 * 10**8, 4 * 10**6),
    )(start, token_mask, lane_hbm, pair_hbm, gain, bias, weight)
    factors = exchange(sent_factors)

    h, coef, normed, mixed, gate_coef = pl.pallas_call(
        side_kernel,
        name="side",
        grid=(tiles,),
        in_specs=[
            smem, smem, lane_spec, cell_spec, cell_spec, row_spec, row_spec,
            whole((channels, 5 * channels)), row_spec, whole((channels, channels)),
        ],
        out_specs=[h_spec, coef_spec, column_spec, column_spec, column_spec],
        out_shape=[
            pltpu.HBM((tiles, channels * rows, LANES), F32),
            pltpu.HBM((tiles, 4, channels, cells), BF16),
            pltpu.HBM((tiles, channels, cells), BF16),
            pltpu.HBM((tiles, channels, cells), BF16),
            pltpu.HBM((tiles, channels, cells), F32),
        ],
        scratch_shapes=[pltpu.VMEM((5 * channels, channels), BF16)],
        compiler_params=params(40),
        cost_estimate=cost(12 * 10**8, 16 * 10**6),
    )(start, token_mask, lane_hbm, pair_hbm, cot_hbm, gain, bias, weight, out_gain, out_weight)
    near = (coef, normed)
    h, coef, normed, mixed, gate_coef = pinned(h, coef, normed, mixed, gate_coef)

    sent_product = pl.pallas_call(
        product_kernel,
        name="product",
        in_specs=[vmem],
        out_specs=anywhere,
        out_shape=pltpu.HBM((slabs, pair * tiles, LANES), BF16),
        scratch_shapes=[
            pltpu.VMEM((4, tokens, tokens), BF16),
            pltpu.VMEM((tiles, slabs, pair, LANES), BF16),
            pltpu.SemaphoreType.DMA((tiles,)),
        ],
        compiler_params=params(20),
        cost_estimate=cost(6 * 10**8, 3 * 10**6),
    )(factors)
    product = exchange(sent_product)

    factor_slab = pl.pallas_call(
        slab_unpack_kernel,
        name="slabs",
        in_specs=[vmem],
        out_specs=whole((4, tokens, tokens)),
        out_shape=pltpu.HBM((4, tokens, tokens), BF16),
        compiler_params=params(20),
        cost_estimate=cost(10**6, 4 * 10**6),
    )(factors)
    (factor_slab,) = pinned(factor_slab)

    sent_grad = pl.pallas_call(
        product_grad_kernel,
        name="product_grad",
        grid=(tiles,),
        in_specs=[vmem, anywhere, anywhere],
        out_specs=wire_spec(pair),
        out_shape=pltpu.HBM((slabs, pair * tiles, LANES), BF16),
        scratch_shapes=[
            pltpu.VMEM((channels * rows, LANES), F32),
            pltpu.VMEM((tiles, channels * rows, LANES), F32),
            pltpu.SemaphoreType.DMA((tiles,)),
        ],
        compiler_params=params(16),
        cost_estimate=cost(10**7, 4 * 10**6),
    )(product, h, factor_slab)
    grad = exchange(sent_grad)

    gate_normed, early_share = pl.pallas_call(
        gate_side_kernel,
        name="gate_side",
        grid=(tiles,),
        in_specs=[
            vmem, column_spec, column_spec, column_spec, row_spec, row_spec,
            whole((channels, channels)),
            pl.BlockSpec((channels, channels), lambda t: (0, 4)),
        ],
        out_specs=[column_spec, whole((slabs, 8, LANES))],
        out_shape=[
            pltpu.HBM((tiles, channels, cells), F32),
            pltpu.HBM((slabs, 8, LANES), BF16),
        ],
        scratch_shapes=[
            pltpu.VMEM((channels * rows, LANES), F32),
            pltpu.VMEM((channels, channels), F32),
            pltpu.VMEM((channels, channels), F32),
            pltpu.VMEM((slabs * 8, LANES), F32),
        ],
        compiler_params=params(24),
        cost_estimate=cost(6 * 10**8, 8 * 10**6),
    )(product, normed, mixed, gate_coef, out_gain, out_bias, out_weight, weight)
    gate_normed, early_share = pinned(gate_normed, early_share)

    height = 2 * pair * tiles
    sent_parts = pl.pallas_call(
        factor_grad_kernel,
        name="factor_grad",
        in_specs=[vmem, anywhere, anywhere],
        out_specs=vmem,
        out_shape=jax.ShapeDtypeStruct((slabs, height, LANES), BF16),
        scratch_shapes=[
            pltpu.VMEM((2, tokens, tokens), BF16),
            pltpu.VMEM((2, tokens, tokens), BF16),
            pltpu.VMEM((4, tokens, tokens), BF16),
            pltpu.SemaphoreType.DMA((4,)),
        ],
        compiler_params=params(20),
        cost_estimate=cost(11 * 10**8, 5 * 10**6),
    )(grad, factor_slab, early_share)
    parts = exchange(sent_parts)

    late_share = pl.pallas_call(
        proj_grad_kernel,
        name="proj_grad",
        grid=(tiles,),
        in_specs=[vmem, vmem, vmem, whole((slabs, 8, LANES))],
        out_specs=whole((slabs, 16, LANES)),
        out_shape=pltpu.HBM((slabs, 16, LANES), BF16),
        scratch_shapes=[
            pltpu.VMEM((2, channels * rows, LANES), F32),
            pltpu.VMEM((4, channels, channels), F32),
            pltpu.VMEM((slabs * 8, LANES), F32),
        ],
        compiler_params=params(24),
        cost_estimate=cost(6 * 10**8, 8 * 10**6),
    )(parts, *near, early_share)
    shares = exchange(late_share)

    pair_gradient = pl.pallas_call(
        pair_grad_kernel,
        name="pair_grad",
        grid=(tiles,),
        in_specs=[vmem, coef_spec, column_spec, cell_spec, row_spec, factor_weight_spec],
        out_specs=cell_spec,
        out_shape=pltpu.HBM((rows, tokens, channels), BF16),
        scratch_shapes=[pltpu.VMEM((2, channels * rows, LANES), F32)],
        compiler_params=params(24),
        cost_estimate=cost(6 * 10**8, 8 * 10**6),
    )(parts, coef, gate_normed, pair_hbm, gain, weight)

    held = channels // slabs
    input_gradient, output_gradient = pl.pallas_call(
        lambda *refs: weight_sum_kernel(*refs, tokens=tokens),
        name="weight_sum",
        in_specs=[vmem],
        out_specs=[whole((held, 5 * channels)), whole((held, channels))],
        out_shape=[
            pltpu.HBM((held, 5 * channels), F32),
            pltpu.HBM((held, channels), F32),
        ],
        compiler_params=params(16),
        cost_estimate=cost(10**5, 4 * 10**5),
    )(shares)
    return (pair_gradient, input_gradient, output_gradient)


def solution(mesh):
    return jax.shard_map(
        on_device,
        mesh=mesh,
        in_specs=(
            P(("cplx", "row"), None, None),
            P(("cplx", "row"), None, None),
            P("cplx"),
            P(),
            P(),
            P(),
            P(),
            P(),
            P(),
        ),
        out_specs=(
            P(("cplx", "row"), None, None),
            P(("cplx", "row"), None),
            P(("cplx", "row"), None),
        ),
        check_vma=False,
    )
```
